256 devices in a mesh: box: 64 (over y, x, z_hi, core), term: 4 (over z_lo).
Axes of the slice: x: 4, y: 4, z: 8 (z_hi: 2, z_lo: 4; z = z_hi * 4 + z_lo), core: 2. Of those that a mesh axis runs over, the one named last changes fastest.
Arguments:
- fine_coeffs: bfloat16 [4, 512, 32, 1024], P(None, 'box'), may hold values from -6 to 6
- fine_blocks: bfloat16 [16, 3, 32, 32], replicated, may hold values from -0.625 to 0.625
- coarse_blocks: bfloat16 [16, 3, 32, 32], replicated, may hold values from -0.625 to 0.625
- two_scale: bfloat16 [32, 64], replicated, may hold values from -0.75 to 0.75
- term_exponent: int32 [8], replicated, may hold values from 0 to 15
Outputs:
- applied: float32 [4, 512, 32, 1024], P(None, ('box', 'term'))
The draws below stay inside these ranges and needn't reach their ends.
All inputs are finite; a program needn't handle non-finite values.
Results may differ from the reference program's by a relative error of at most 0.0047.
Values may be sent and summed in bfloat16 or wider, within the bound.
No kernel may reach another device: no remote copies, remote signals or barrier semaphores. Data moves between devices by JAX's collectives and lax.ppermute only.
A program may use at most 128 MiB of HBM per device.

```python
import jax
import jax.numpy as jnp
import numpy as np
from jax import lax

K = 32
FUNCS = 4
TERMS = 8
EXPS = 16
G = 4
NPAR = 64
NFINE = 512


def plant(entries, key, smallest, largest):
    shape = entries.shape
    index_at = [jax.random.randint(jax.random.fold_in(key, axis), (), 0, shape[axis]) for axis in range(len(shape))]
    entries = entries.at[tuple(index_at)].set(smallest)
    longest = shape.index(max(shape))
    index_at[longest] = (index_at[longest] + 1) % shape[longest]
    return entries.at[tuple(index_at)].set(largest)


def level_of(stream_key, dims, cuts, smallest, top_value):
    def one(position, parts):
        draws = jax.random.uniform(jax.random.fold_in(jax.random.fold_in(stream_key, 6), position), (parts,), jnp.float32, smallest / len(cuts), top_value / len(cuts))
        return jnp.repeat(jnp.exp(draws), dims[position] // parts).reshape((-1,) + (1,) * (len(dims) - position - 1))

    level = one(*cuts[0])
    for cut in cuts[1:]:
        level = level * one(*cut)
    return level


def noise(key, dims, deviation, bound, cuts=(), held_as=jnp.bfloat16):
    factor_of = level_of(key, dims, cuts, -0.22, 0.18) if cuts else 1.0
    values = jax.random.normal(key, dims, jnp.float32) * deviation * factor_of
    return jnp.minimum(jnp.maximum(values, -bound), bound).astype(held_as)


def setup_inputs(seed: int = 0) -> dict:
    splits = jax.random.split(jax.random.key(seed), 6)
    fine_coeffs = noise(splits[0], (FUNCS, NFINE, K, K * K), 1.0, 6.0, ((1, 64),))
    fine_blocks = noise(splits[1], (EXPS, 3, K, K), (3 * K) ** -0.5, 0.625)
    coarse_blocks = noise(splits[2], (EXPS, 3, K, K), (3 * K) ** -0.5, 0.625)
    two_scale = noise(splits[3], (K, 2 * K), (2 * K) ** -0.5, 0.75)
    term_exponent = plant(jax.random.randint(splits[4], (TERMS,), 0, EXPS), jax.random.fold_in(splits[4], 1), 0, EXPS - 1).astype(jnp.int32)
    return dict(fine_coeffs=fine_coeffs, fine_blocks=fine_blocks, coarse_blocks=coarse_blocks, two_scale=two_scale, term_exponent=term_exponent)


def to_cells(fine_coeffs):
    functions = fine_coeffs.shape[0]
    breadth = fine_coeffs.shape[2]
    cube = fine_coeffs.reshape(functions, NPAR, 2, 2, 2, breadth, breadth, breadth)
    cube = cube.transpose(0, 1, 2, 5, 3, 6, 4, 7)
    return cube.reshape(functions, NPAR, 2 * breadth, 2 * breadth, 2 * breadth)


def from_cells(values):
    functions = values.shape[0]
    breadth = K
    cube = values.reshape(functions, NPAR, 2, breadth, 2, breadth, 2, breadth)
    cube = cube.transpose(0, 1, 2, 4, 6, 3, 5, 7)
    return cube.reshape(functions, NPAR * 8, breadth, breadth * breadth)


def chain_apply(chain, blocks):
    layout = chain.shape
    breadth = layout[-1]
    flattened = chain.reshape(-1, breadth)
    pieces = [jnp.dot(flattened, blocks[offset], preferred_element_type=jnp.float32).reshape(layout) for offset in range(3)]
    return pieces[1] + jnp.roll(pieces[0], 1, axis=-2) + jnp.roll(pieces[2], -1, axis=-2)


def one_pass(values, blocks, along_axis, factor):
    functions = values.shape[0]
    edge = values.shape[2]
    breadth = blocks.shape[-1]
    if along_axis == 4:
        split = (functions, NPAR, edge, edge, factor, breadth)
        order = (0, 2, 3, 1, 4, 5)
    elif along_axis == 3:
        split = (functions, G * G, G, edge, factor, breadth, edge)
        order = (0, 2, 3, 6, 1, 4, 5)
    else:
        split = (functions, G, G * G, factor, breadth, edge, edge)
        order = (0, 2, 5, 6, 1, 3, 4)
    moved = values.reshape(split).transpose(order)
    moved_shape = moved.shape
    chain = moved.reshape(moved_shape[:-3] + (moved_shape[-3] * moved_shape[-2], breadth))
    result = chain_apply(chain, blocks).reshape(moved_shape)
    back = tuple(int(v) for v in np.argsort(np.array(order)))
    return result.transpose(back).reshape(values.shape)


def operate(values, blocks, factor):
    for along_axis in (4, 3, 2):
        values = one_pass(values, blocks, along_axis, factor)
        if along_axis != 2:
            values = values.astype(jnp.bfloat16)
    return values


def reference(fine_coeffs, fine_blocks, coarse_blocks, two_scale, term_exponent):
    fine_cells = to_cells(fine_coeffs)
    parents = jnp.einsum("fpxyz,kz->fpxyk", fine_cells, two_scale, preferred_element_type=jnp.float32).astype(jnp.bfloat16)
    parents = jnp.einsum("fpxyk,jy->fpxjk", parents, two_scale, preferred_element_type=jnp.float32).astype(jnp.bfloat16)
    parents = jnp.einsum("fpxjk,ix->fpijk", parents, two_scale, preferred_element_type=jnp.float32).astype(jnp.bfloat16)
    fine_sum = jnp.zeros(fine_cells.shape, jnp.float32)
    coarse_sum = jnp.zeros(parents.shape, jnp.float32)
    for term_index in range(TERMS):
        chosen = term_exponent[term_index]
        fine_sum = fine_sum + operate(fine_cells, jnp.take(fine_blocks, chosen, axis=0), 2)
        coarse_sum = coarse_sum + operate(parents, jnp.take(coarse_blocks, chosen, axis=0), 1)
    exact_mode = lax.Precision.HIGHEST
    scale_wide = two_scale.astype(jnp.float32)
    spread_out = jnp.einsum("fpijk,kz->fpijz", coarse_sum, scale_wide, precision=exact_mode)
    spread_out = jnp.einsum("fpijz,jy->fpiyz", spread_out, scale_wide, precision=exact_mode)
    spread_out = jnp.einsum("fpiyz,ix->fpxyz", spread_out, scale_wide, precision=exact_mode)
    return from_cells(fine_sum + spread_out)
```

```python
import jax
import jax.numpy as jnp
from jax import lax
from jax.experimental import pallas as pl
from jax.experimental.pallas import tpu as pltpu
from jax.sharding import PartitionSpec as P

BF = jnp.bfloat16
F32 = jnp.float32
INTERPRET = False
PARAMS = dict(compiler_params=pltpu.CompilerParams(vmem_limit_bytes=56 * 1024 * 1024))


def dot(a, b):
    return jnp.dot(a, b, preferred_element_type=F32)


def dot_t(a, b):
    return lax.dot_general(a, b, (((1,), (1,)), ((), ())), preferred_element_type=F32)


def split(value):
    hi = value.astype(BF)
    return hi, (value - hi.astype(F32)).astype(BF)


def call(kernel, outs, scratch=(), name=None):
    return pl.pallas_call(
        kernel,
        out_shape=outs,
        scratch_shapes=list(scratch),
        interpret=INTERPRET,
        name=name,
        **PARAMS,
    )


def lane_eye(count):
    return jnp.eye(count, dtype=BF)


def fine_weights(fb):
    placed = jnp.stack(
        [jnp.pad(fb, ((0, 0), (0, 1), (0, 0), (0, 0))), jnp.pad(fb, ((0, 0), (1, 0), (0, 0), (0, 0)))],
        axis=3,
    )
    wz = (
        placed[:, :, None, :, None] * lane_eye(4)[None, None, :, None, :, None, None]
    ).reshape(8, 512, 256)
    wx = placed.transpose(0, 3, 4, 1, 2).reshape(8, 64, 128)
    flipped = fb[:, ::-1]
    spread = jnp.stack(
        [jnp.pad(flipped, ((0, 0), (0, 1), (0, 0), (0, 0))), jnp.pad(flipped, ((0, 0), (1, 0), (0, 0), (0, 0)))],
        axis=1,
    )
    my = spread.reshape(8, 2, 4, 16, 2, 32).transpose(4, 2, 5, 0, 1, 3).reshape(256, 256)
    return wz, wx, my


def coarse_weights(cb):
    wz = (
        cb[:, :, None, :, None, :] * lane_eye(4)[None, None, :, None, :, None]
    ).reshape(4, 2, 384, 128).transpose(0, 2, 1, 3).reshape(4, 384, 256)
    wx = cb.transpose(0, 3, 1, 2).reshape(8, 32, 96)
    my = cb[:, ::-1].reshape(8, 3, 8, 4, 32).transpose(3, 1, 4, 0, 2).reshape(384, 64)
    return wz, wx, my


def scale_weights(two_scale):
    fz = (
        two_scale.T.reshape(2, 1, 32, 1, 32) * lane_eye(4)[None, :, None, :, None]
    ).reshape(256, 128)
    ky = (two_scale.T[:, None, :, None] * lane_eye(32)[None, :, None, :]).reshape(2048, 1024)
    st2 = jnp.concatenate([two_scale.T, two_scale.T], axis=1)
    return fz, ky, st2


def parent_kernel(own, fz, ky, s, out, rows, wide):
    for yg in range(16):
        cy, g = divmod(yg, 8)
        for cx in range(2):
            for cz in range(2):
                rows[yg * 64 + cx * 32 : yg * 64 + cx * 32 + 32, cz * 128 : cz * 128 + 128] = own[
                    4 * cx + 2 * cy + cz, :, g * 128 : g * 128 + 128
                ]
    along_z = dot(rows[...], fz[...]).astype(BF)
    for yg in range(16):
        wide[:, yg * 128 : yg * 128 + 128] = along_z[yg * 64 : yg * 64 + 64]
    along_y = dot(wide[...], ky[...]).astype(BF)
    out[...] = dot(s[...], along_y).astype(BF)


def parents_of(own, fz, ky, s):
    return call(
        parent_kernel,
        jax.ShapeDtypeStruct((32, 1024), BF),
        [pltpu.VMEM((1024, 256), BF), pltpu.VMEM((64, 2048), BF)],
        "parents",
    )(own, fz, ky, s)


def main_kernel(
    own, zm, zp, xm_own, xp_own, xm_far, xp_far, par, czm, czp,
    wz, wx, my, cwz, cwx, cmy,
    out, send_up, send_dn, out_c,
    left, mid, wide, done, left_c, mid_c, wide_c, done_c,
):
    for cy in range(2):
        sources = [
            [xm_far[cy], xm_own[2 * cy], xm_own[2 * cy + 1], xm_far[2 + cy]],
            [zm[cy], own[2 * cy], own[2 * cy + 1], zp[cy]],
            [zm[2 + cy], own[4 + 2 * cy], own[5 + 2 * cy], zp[2 + cy]],
            [xp_far[cy], xp_own[2 * cy], xp_own[2 * cy + 1], xp_far[2 + cy]],
        ]
        for xb in range(4):
            for zb in range(4):
                box = sources[xb][zb]
                for g in range(8):
                    row = (cy * 8 + g) * 128 + xb * 32
                    left[row : row + 32, zb * 128 : zb * 128 + 128] = box[:, g * 128 : g * 128 + 128]

    def fine_term(t, carry):
        weight = wz[t]
        for m in range(4):
            passed = dot(left[m * 512 : m * 512 + 512, :], weight).astype(BF)
            mid[m * 4 : m * 4 + 4] = passed.reshape(4, 128, 256)
        weight_x = wx[t]
        for yg in range(16):
            passed = dot(weight_x, mid[yg])
            base = (t * 32 + 2 * yg) * 64
            wide[pl.ds(base, 64), :] = passed[:, :128]
            wide[pl.ds(base + 64, 64), :] = passed[:, 128:]
        return carry

    lax.fori_loop(0, 8, fine_term, 0)

    def fine_rows(k, carry):
        u = 2 * k
        data = jnp.concatenate(
            [wide[pl.ds(u, 256, stride=64), :].astype(BF), wide[pl.ds(u + 1, 256, stride=64), :].astype(BF)], axis=1
        )
        passed = dot(my[...], data)
        for i in range(2):
            lanes = passed[:, i * 128 : i * 128 + 128]
            base = pl.multiple_of((u + i) * 128, 128)
            done[pl.ds(base, 128), :] = lanes[:128] + pltpu.roll(lanes[128:], 64, 1)
        return carry

    lax.fori_loop(0, 32, fine_rows, 0)

    lane64 = lax.broadcasted_iota(jnp.int32, (64, 128), 1) // 32

    def fine_lanes(g, carry):
        at = pl.multiple_of(g * 128, 128)
        for vb in range(4):
            parts = [done[pl.ds(vb * 32 + 4 * g + j, 64, stride=128), :] for j in range(4)]
            for cz in range(2):
                block = parts[0] if cz == 0 else pltpu.roll(parts[0], 96, 1)
                for j in range(1, 4):
                    turn = (32 * (j - cz)) % 128
                    moved = pltpu.roll(parts[j], turn, 1) if turn else parts[j]
                    block = jnp.where(lane64 == j, moved, block)
                for cx in range(2):
                    piece = block[cx * 32 : cx * 32 + 32]
                    if vb == 0:
                        send_dn[2 * cx + cz, :, pl.ds(at, 128)] = piece.astype(BF)
                    elif vb == 3:
                        send_up[2 * cx + cz, :, pl.ds(at, 128)] = piece.astype(BF)
                    else:
                        out[4 * cx + 2 * (vb - 1) + cz, :, pl.ds(at, 128)] = piece
        return carry

    lax.fori_loop(0, 8, fine_lanes, 0)

    sources = [
        [xm_far[5], xm_far[4], xm_far[6]],
        [czm[...], par[...], czp[...]],
        [xp_far[5], xp_far[4], xp_far[6]],
    ]
    for xb in range(3):
        for zb in range(3):
            for g in range(8):
                row = g * 96 + xb * 32
                left_c[row : row + 32, zb * 128 : zb * 128 + 128] = sources[xb][zb][:, g * 128 : g * 128 + 128]

    def coarse_pair(h, carry):
        passed = dot(left_c[...], cwz[h]).astype(BF)
        mid_c[...] = passed.reshape(8, 96, 256)
        for i in range(2):
            weight_x = cwx[2 * h + i]
            for g in range(0, 8, 2):
                data = jnp.concatenate(
                    [mid_c[g, :, i * 128 : i * 128 + 128], mid_c[g + 1, :, i * 128 : i * 128 + 128]], axis=1
                )
                moved = dot(weight_x, data)
                base = ((2 * h + i) * 8 + g) * 32
                wide_c[pl.ds(base, 32), :] = moved[:, :128]
                wide_c[pl.ds(base + 32, 32), :] = moved[:, 128:]
        return carry

    lax.fori_loop(0, 4, coarse_pair, 0)

    def coarse_rows(k, carry):
        u = 2 * k
        data = jnp.concatenate(
            [wide_c[pl.ds(u, 64, stride=32), :].astype(BF), wide_c[pl.ds(u + 1, 64, stride=32), :].astype(BF)], axis=1
        )
        passed = dot(cmy[...], data)
        for i in range(2):
            lanes = passed[:, i * 128 : i * 128 + 128]
            total = lanes[:96]
            for j in range(1, 4):
                total = total + pltpu.roll(lanes[j * 96 : j * 96 + 96], 128 - 32 * j, 1)
            base = pl.multiple_of((u + i) * 96, 32)
            done_c[pl.ds(base, 96), :] = total
        return carry

    lax.fori_loop(0, 16, coarse_rows, 0)

    lane32 = lax.broadcasted_iota(jnp.int32, (32, 128), 1) // 32

    def coarse_lanes(g, carry):
        at = pl.multiple_of(g * 128, 128)
        for vb in range(3):
            block = done_c[pl.ds(vb * 32 + 4 * g, 32, stride=96), :]
            for j in range(1, 4):
                part = done_c[pl.ds(vb * 32 + 4 * g + j, 32, stride=96), :]
                block = jnp.where(lane32 == j, pltpu.roll(part, 32 * j, 1), block)
            if vb == 0:
                send_dn[4, :, pl.ds(at, 128)] = block.astype(BF)
            elif vb == 2:
                send_up[4, :, pl.ds(at, 128)] = block.astype(BF)
            else:
                out_c[:, pl.ds(at, 128)] = block
        return carry

    lax.fori_loop(0, 8, coarse_lanes, 0)


def passes(*operands):
    return call(
        main_kernel,
        (
            jax.ShapeDtypeStruct((8, 32, 1024), F32),
            jax.ShapeDtypeStruct((5, 32, 1024), BF),
            jax.ShapeDtypeStruct((5, 32, 1024), BF),
            jax.ShapeDtypeStruct((32, 1024), F32),
        ),
        [
            pltpu.VMEM((2048, 512), BF),
            pltpu.VMEM((16, 128, 256), BF),
            pltpu.VMEM((16384, 128), F32),
            pltpu.VMEM((8192, 128), F32),
            pltpu.VMEM((768, 384), BF),
            pltpu.VMEM((8, 96, 256), BF),
            pltpu.VMEM((2048, 128), F32),
            pltpu.VMEM((3072, 128), F32),
        ],
        "passes",
    )(*operands)


def final_kernel(own, own_c, low, high, fz, ky, st2, out, rows, mixed, deep):
    total = own_c[...] + low[4].astype(F32) + high[4].astype(F32)
    hi, lo = split(total)
    for g in range(8):
        rows[g * 64 : g * 64 + 32, :] = hi[:, g * 128 : g * 128 + 128]
        rows[g * 64 + 32 : g * 64 + 64, :] = lo[:, g * 128 : g * 128 + 128]
    along_z = dot_t(rows[...], fz[...])
    for g in range(8):
        both = along_z[g * 64 : g * 64 + 32] + along_z[g * 64 + 32 : g * 64 + 64]
        hi, lo = split(both)
        for cz in range(2):
            mixed[cz * 64 : cz * 64 + 32, g * 128 : g * 128 + 128] = hi[:, cz * 128 : cz * 128 + 128]
            mixed[cz * 64 + 32 : cz * 64 + 64, g * 128 : g * 128 + 128] = lo[:, cz * 128 : cz * 128 + 128]
    along_y = dot_t(mixed[...], ky[...])
    for cz in range(2):
        hi, lo = split(along_y[cz * 64 : cz * 64 + 32] + along_y[cz * 64 + 32 : cz * 64 + 64])
        deep[:32, :] = hi
        deep[32:, :] = lo
        along_x = dot(st2[...], deep[...])
        for cx in range(2):
            for cy in range(2):
                added = (low if cy == 0 else high)[2 * cx + cz].astype(F32)
                spread = along_x[cx * 32 : cx * 32 + 32, cy * 1024 : cy * 1024 + 1024]
                box = 4 * cx + 2 * cy + cz
                out[box] = (own[box] + spread + added).astype(BF)


def finish(*operands):
    return call(
        final_kernel,
        jax.ShapeDtypeStruct((8, 32, 1024), BF),
        [pltpu.VMEM((512, 128), BF), pltpu.VMEM((128, 1024), BF), pltpu.VMEM((64, 2048), BF)],
        "finish",
    )(*operands)


def shift(block, distance):
    count = lax.axis_size("box")
    return lax.ppermute(block, "box", [(i, (i + distance) % count) for i in range(count)])


def crosses(p, step):
    return (p % 2 == 1) if step == 1 else (p % 2 == 0)


def shift_z(block, step):
    boxes, groups = lax.axis_size("box"), lax.axis_size("term")
    route = []
    for p in range(boxes):
        for t in range(groups):
            to = groups - 1 - t if crosses(p, step) else t
            route.append((p * groups + t, ((p + step) % boxes) * groups + to))
    return lax.ppermute(block, ("box", "term"), route)


def z_layer(fine_coeffs, step, p, t):
    other = lax.axis_size("term") - 1 - t
    cross = (p % 2 == 1) if step == 1 else (p % 2 == 0)
    chosen = lax.dynamic_index_in_dim(fine_coeffs, jnp.where(cross, other, t), 0, False)
    layer = chosen.reshape(4, 2, 32, 1024)[:, 1 if step == 1 else 0]
    return shift_z(layer, step)


def on_device(fine_coeffs, fine_blocks, coarse_blocks, two_scale, term_exponent):
    p = lax.axis_index("box")
    t = lax.axis_index("term")
    zm = z_layer(fine_coeffs, 1, p, t)
    zp = z_layer(fine_coeffs, -1, p, t)
    own = lax.dynamic_index_in_dim(fine_coeffs, t, 0, False)
    xm_own = shift(own[4:], 16)
    xp_own = shift(own[:4], -16)

    fz, ky, st2 = scale_weights(two_scale)
    par = parents_of(own, fz, ky, two_scale)
    czm = shift(par, 1)
    czp = shift(par, -1)

    far_up = jnp.concatenate([zm[2:], zp[2:], par[None], czm[None], czp[None]], axis=0)
    far_dn = jnp.concatenate([zm[:2], zp[:2], par[None], czm[None], czp[None]], axis=0)
    xm_far = shift(far_up, 16)
    xp_far = shift(far_dn, -16)

    wz, wx, my = fine_weights(jnp.take(fine_blocks, term_exponent, axis=0))
    cwz, cwx, cmy = coarse_weights(jnp.take(coarse_blocks, term_exponent, axis=0))
    out, send_up, send_dn, out_c = passes(
        own, zm, zp, xm_own, xp_own, xm_far, xp_far, par, czm, czp, wz, wx, my, cwz, cwx, cmy
    )
    low = shift(send_up, 4)
    high = shift(send_dn, -4)
    total = finish(out, out_c, low, high, fz, ky, st2)
    groups = lax.axis_size("term")
    mine = lax.all_to_all(total.reshape(groups, 2, 32, 1024), "term", 0, 0)
    return mine.astype(F32)


def solution(mesh):
    placed = (P(None, "box", None, None), P(), P(), P(), P())
    return jax.shard_map(
        on_device,
        mesh=mesh,
        in_specs=placed,
        out_specs=P(None, ("box", "term"), None, None),
        check_vma=False,
    )
```

```python
import jax
import jax.numpy as jnp
from jax import lax
from jax.experimental import pallas as pl
from jax.experimental.pallas import tpu as pltpu
from jax.sharding import PartitionSpec as P


BF = jnp.bfloat16
F32 = jnp.float32
INTERPRET = False
PARAMS = dict(compiler_params=pltpu.CompilerParams(vmem_limit_bytes=56 * 1024 * 1024))


def dot(a, b):
    return jnp.dot(a, b, preferred_element_type=F32)


def dot_t(a, b):
    return lax.dot_general(a, b, (((1,), (1,)), ((), ())), preferred_element_type=F32)


def split(value):
    hi = value.astype(BF)
    return hi, (value - hi.astype(F32)).astype(BF)


def call(kernel, outs, scratch=()):
    return pl.pallas_call(kernel, out_shape=outs, scratch_shapes=list(scratch), interpret=INTERPRET, **PARAMS)


def same(rows, columns, test):
    i = lax.broadcasted_iota(jnp.int32, (rows, columns), 0)
    j = lax.broadcasted_iota(jnp.int32, (rows, columns), 1)
    return test(i, j).astype(F32).astype(BF)


def weight_kernel(
    exponents, fine, coarse,
    wz, wx, my, cwz, cwx, cmy,
    dense, turned, tall, dense_c, turned_c, tall_c,
):
    wz[...] = jnp.zeros(wz.shape, BF)
    cwz[...] = jnp.zeros(cwz.shape, BF)
    dense[...] = jnp.zeros(dense.shape, F32)
    turned[...] = jnp.zeros(turned.shape, F32)
    eye = same(128, 128, lambda i, j: i == j)
    by_parity = same(64, 64, lambda i, j: j == 2 * (i % 32) + i // 32)
    by_four = same(32, 32, lambda i, j: j == 4 * (i % 8) + i // 8)

    def term(t, carry):
        e = exponents[t]
        for d in range(3):
            block = fine[e, d]
            for child in range(2):
                source = d + child
                for y in range(4):
                    row, column = source * 128 + y * 32, y * 64 + child * 32
                    wz[t, row : row + 32, column : column + 32] = block
                wide_block = block.astype(F32)
                dense[source * 32 : source * 32 + 32, child * 32 : child * 32 + 32] = wide_block
                target = 2 + child - d
                turned[child * 32 : child * 32 + 32, target * 32 : target * 32 + 32] = wide_block
        wx[t] = dot_t(eye[:64, :64], dense[...].astype(BF)).astype(BF)
        chosen = dot(by_parity, turned[...].astype(BF))
        for parity in range(2):
            tall[parity, pl.ds(t * 32, 32), :] = chosen[parity * 32 : parity * 32 + 32]
        for d in range(3):
            block = coarse[e, d]
            dense_c[d * 32 : d * 32 + 32, :] = block.astype(F32)
            turned_c[:, (2 - d) * 32 : (2 - d) * 32 + 32] = block.astype(F32)
            for y in range(4):
                cwz[t, d * 128 + y * 32 : d * 128 + y * 32 + 32, y * 32 : y * 32 + 32] = block
        cwx[t] = dot_t(eye[:32, :32], dense_c[...].astype(BF)).astype(BF)
        chosen = dot(by_four, turned_c[...].astype(BF))
        for parity in range(4):
            tall_c[parity, pl.ds(t * 8, 8), :] = chosen[parity * 8 : parity * 8 + 8]
        return carry

    lax.fori_loop(0, 8, term, 0)
    for parity in range(2):
        my[parity * 128 : parity * 128 + 128, :] = dot_t(eye, tall[parity].astype(BF)).astype(BF)
    for parity in range(4):
        cmy[parity * 96 : parity * 96 + 96, :] = dot_t(eye[:96, :96], tall_c[parity].astype(BF)).astype(BF)


def weights(exponents, fine, coarse):
    whole = pl.BlockSpec(memory_space=pltpu.VMEM)
    return pl.pallas_call(
        weight_kernel,
        out_shape=(
            jax.ShapeDtypeStruct((8, 512, 256), BF),
            jax.ShapeDtypeStruct((8, 64, 128), BF),
            jax.ShapeDtypeStruct((256, 256), BF),
            jax.ShapeDtypeStruct((8, 384, 128), BF),
            jax.ShapeDtypeStruct((8, 32, 96), BF),
            jax.ShapeDtypeStruct((384, 64), BF),
        ),
        in_specs=[pl.BlockSpec(memory_space=pltpu.SMEM), whole, whole],
        scratch_shapes=[
            pltpu.VMEM((128, 64), F32),
            pltpu.VMEM((64, 128), F32),
            pltpu.VMEM((2, 256, 128), F32),
            pltpu.VMEM((96, 32), F32),
            pltpu.VMEM((32, 96), F32),
            pltpu.VMEM((4, 64, 96), F32),
        ],
        interpret=INTERPRET,
        name="weights",
        **PARAMS,
    )(exponents, fine, coarse)


def parent_kernel(own, s, out, fz, ky, st2, rows, wide):
    scale = s[...]
    tiled = lax.dot_general(
        scale, same(32, 128, lambda i, j: j % 32 == i), (((0,), (0,)), ((), ())), preferred_element_type=F32
    )
    block = same(128, 128, lambda i, j: i // 32 == j // 32).astype(F32)
    for cz in range(2):
        part = tiled[cz * 32 : cz * 32 + 32]
        fz[cz * 128 : cz * 128 + 128, :] = (jnp.concatenate([part] * 4, axis=0) * block).astype(BF)
    st2[...] = lax.dot_general(
        scale, same(32, 64, lambda i, j: j % 32 == i), (((0,), (0,)), ((), ())), preferred_element_type=F32
    ).astype(BF)
    spread = lax.dot_general(
        scale, same(32, 1024, lambda i, j: j // 32 == i), (((0,), (0,)), ((), ())), preferred_element_type=F32
    )
    lane = lax.broadcasted_iota(jnp.int32, (32, 1024), 1) % 32 == lax.broadcasted_iota(jnp.int32, (32, 1024), 0)
    for y in range(64):
        ky[y * 32 : y * 32 + 32, :] = jnp.where(
            lane, jnp.broadcast_to(spread[y : y + 1], (32, 1024)), 0.0
        ).astype(BF)
    for yg in range(16):
        cy, g = divmod(yg, 8)
        for cx in range(2):
            for cz in range(2):
                rows[yg * 64 + cx * 32 : yg * 64 + cx * 32 + 32, cz * 128 : cz * 128 + 128] = own[
                    4 * cx + 2 * cy + cz, :, g * 128 : g * 128 + 128
                ]
    along_z = dot(rows[...], fz[...]).astype(BF)
    for yg in range(16):
        wide[:, yg * 128 : yg * 128 + 128] = along_z[yg * 64 : yg * 64 + 64]
    along_y = dot(wide[...], ky[...]).astype(BF)
    out[...] = dot(scale, along_y).astype(BF)


def parents_of(own, s):
    return call(
        parent_kernel,
        (
            jax.ShapeDtypeStruct((32, 1024), BF),
            jax.ShapeDtypeStruct((256, 128), BF),
            jax.ShapeDtypeStruct((2048, 1024), BF),
            jax.ShapeDtypeStruct((64, 64), BF),
        ),
        [pltpu.VMEM((1024, 256), BF), pltpu.VMEM((64, 2048), BF)],
    )(own, s)


def main_kernel(
    own, zm, zp, xm_own, xp_own, xm_far, xp_far, par, czm, czp,
    wz, wx, my, cwz, cwx, cmy,
    out, send_up, send_dn, out_c,
    left, mid, wide, done, left_c, mid_c, wide_c, done_c,
):
    for cy in range(2):
        sources = [
            [xm_far[cy], xm_own[2 * cy], xm_own[2 * cy + 1], xm_far[2 + cy]],
            [zm[cy], own[2 * cy], own[2 * cy + 1], zp[cy]],
            [zm[2 + cy], own[4 + 2 * cy], own[5 + 2 * cy], zp[2 + cy]],
            [xp_far[cy], xp_own[2 * cy], xp_own[2 * cy + 1], xp_far[2 + cy]],
        ]
        for xb in range(4):
            for zb in range(4):
                box = sources[xb][zb]
                for g in range(8):
                    row = (cy * 8 + g) * 128 + xb * 32
                    left[row : row + 32, zb * 128 : zb * 128 + 128] = box[:, g * 128 : g * 128 + 128]

    def fine_term(t, carry):
        weight = wz[t]
        for m in range(4):
            passed = dot(left[m * 512 : m * 512 + 512, :], weight).astype(BF)
            mid[m * 4 : m * 4 + 4] = passed.reshape(4, 128, 256)
        weight_x = wx[t]
        for yg in range(16):
            passed = dot(weight_x, mid[yg])
            base = (t * 32 + 2 * yg) * 64
            wide[pl.ds(base, 64), :] = passed[:, :128]
            wide[pl.ds(base + 64, 64), :] = passed[:, 128:]
        return carry

    lax.fori_loop(0, 8, fine_term, 0)

    def fine_rows(k, carry):
        u = 2 * k
        data = jnp.concatenate(
            [wide[pl.ds(u, 256, stride=64), :].astype(BF), wide[pl.ds(u + 1, 256, stride=64), :].astype(BF)], axis=1
        )
        passed = dot(my[...], data)
        for i in range(2):
            lanes = passed[:, i * 128 : i * 128 + 128]
            base = pl.multiple_of((u + i) * 128, 128)
            done[pl.ds(base, 128), :] = lanes[:128] + pltpu.roll(lanes[128:], 64, 1)
        return carry

    lax.fori_loop(0, 32, fine_rows, 0)

    lane64 = lax.broadcasted_iota(jnp.int32, (64, 128), 1) // 32

    def fine_lanes(g, carry):
        at = pl.multiple_of(g * 128, 128)
        for vb in range(4):
            parts = [done[pl.ds(vb * 32 + 4 * g + j, 64, stride=128), :] for j in range(4)]
            for cz in range(2):
                block = parts[0] if cz == 0 else pltpu.roll(parts[0], 96, 1)
                for j in range(1, 4):
                    turn = (32 * (j - cz)) % 128
                    moved = pltpu.roll(parts[j], turn, 1) if turn else parts[j]
                    block = jnp.where(lane64 == j, moved, block)
                for cx in range(2):
                    piece = block[cx * 32 : cx * 32 + 32]
                    if vb == 0:
                        send_dn[2 * cx + cz, :, pl.ds(at, 128)] = piece.astype(BF)
                    elif vb == 3:
                        send_up[2 * cx + cz, :, pl.ds(at, 128)] = piece.astype(BF)
                    else:
                        out[4 * cx + 2 * (vb - 1) + cz, :, pl.ds(at, 128)] = piece
        return carry

    lax.fori_loop(0, 8, fine_lanes, 0)

    sources = [
        [xm_far[5], xm_far[4], xm_far[6]],
        [czm[...], par[...], czp[...]],
        [xp_far[5], xp_far[4], xp_far[6]],
    ]
    for xb in range(3):
        for zb in range(3):
            for g in range(8):
                row = g * 96 + xb * 32
                left_c[row : row + 32, zb * 128 : zb * 128 + 128] = sources[xb][zb][:, g * 128 : g * 128 + 128]

    def coarse_pair(h, carry):
        weight = jnp.concatenate([cwz[2 * h], cwz[2 * h + 1]], axis=1)
        passed = dot(left_c[...], weight).astype(BF)
        mid_c[...] = passed.reshape(8, 96, 256)
        for i in range(2):
            weight_x = cwx[2 * h + i]
            for g in range(0, 8, 2):
                data = jnp.concatenate(
                    [mid_c[g, :, i * 128 : i * 128 + 128], mid_c[g + 1, :, i * 128 : i * 128 + 128]], axis=1
                )
                moved = dot(weight_x, data)
                base = ((2 * h + i) * 8 + g) * 32
                wide_c[pl.ds(base, 32), :] = moved[:, :128]
                wide_c[pl.ds(base + 32, 32), :] = moved[:, 128:]
        return carry

    lax.fori_loop(0, 4, coarse_pair, 0)

    def coarse_rows(k, carry):
        u = 2 * k
        data = jnp.concatenate(
            [wide_c[pl.ds(u, 64, stride=32), :].astype(BF), wide_c[pl.ds(u + 1, 64, stride=32), :].astype(BF)], axis=1
        )
        passed = dot(cmy[...], data)
        for i in range(2):
            lanes = passed[:, i * 128 : i * 128 + 128]
            total = lanes[:96]
            for j in range(1, 4):
                total = total + pltpu.roll(lanes[j * 96 : j * 96 + 96], 128 - 32 * j, 1)
            base = pl.multiple_of((u + i) * 96, 32)
            done_c[pl.ds(base, 96), :] = total
        return carry

    lax.fori_loop(0, 16, coarse_rows, 0)

    lane32 = lax.broadcasted_iota(jnp.int32, (32, 128), 1) // 32

    def coarse_lanes(g, carry):
        at = pl.multiple_of(g * 128, 128)
        for vb in range(3):
            block = done_c[pl.ds(vb * 32 + 4 * g, 32, stride=96), :]
            for j in range(1, 4):
                part = done_c[pl.ds(vb * 32 + 4 * g + j, 32, stride=96), :]
                block = jnp.where(lane32 == j, pltpu.roll(part, 32 * j, 1), block)
            if vb == 0:
                send_dn[4, :, pl.ds(at, 128)] = block.astype(BF)
            elif vb == 2:
                send_up[4, :, pl.ds(at, 128)] = block.astype(BF)
            else:
                out_c[:, pl.ds(at, 128)] = block
        return carry

    lax.fori_loop(0, 8, coarse_lanes, 0)


def passes(*operands):
    return call(
        main_kernel,
        (
            jax.ShapeDtypeStruct((8, 32, 1024), F32),
            jax.ShapeDtypeStruct((5, 32, 1024), BF),
            jax.ShapeDtypeStruct((5, 32, 1024), BF),
            jax.ShapeDtypeStruct((32, 1024), F32),
        ),
        [
            pltpu.VMEM((2048, 512), BF),
            pltpu.VMEM((16, 128, 256), BF),
            pltpu.VMEM((16384, 128), F32),
            pltpu.VMEM((8192, 128), F32),
            pltpu.VMEM((768, 384), BF),
            pltpu.VMEM((8, 96, 256), BF),
            pltpu.VMEM((2048, 128), F32),
            pltpu.VMEM((3072, 128), F32),
        ],
    )(*operands)


def final_kernel(own, own_c, low, high, fz, ky, st2, out, rows, mixed, deep):
    total = own_c[...] + low[4].astype(F32) + high[4].astype(F32)
    hi, lo = split(total)
    for g in range(8):
        rows[g * 64 : g * 64 + 32, :] = hi[:, g * 128 : g * 128 + 128]
        rows[g * 64 + 32 : g * 64 + 64, :] = lo[:, g * 128 : g * 128 + 128]
    along_z = dot_t(rows[...], fz[...])
    for g in range(8):
        both = along_z[g * 64 : g * 64 + 32] + along_z[g * 64 + 32 : g * 64 + 64]
        hi, lo = split(both)
        for cz in range(2):
            mixed[cz * 64 : cz * 64 + 32, g * 128 : g * 128 + 128] = hi[:, cz * 128 : cz * 128 + 128]
            mixed[cz * 64 + 32 : cz * 64 + 64, g * 128 : g * 128 + 128] = lo[:, cz * 128 : cz * 128 + 128]
    along_y = dot_t(mixed[...], ky[...])
    for cz in range(2):
        hi, lo = split(along_y[cz * 64 : cz * 64 + 32] + along_y[cz * 64 + 32 : cz * 64 + 64])
        deep[:32, :] = hi
        deep[32:, :] = lo
        along_x = dot(st2[...], deep[...])
        for cx in range(2):
            for cy in range(2):
                added = (low if cy == 0 else high)[2 * cx + cz].astype(F32)
                spread = along_x[cx * 32 : cx * 32 + 32, cy * 1024 : cy * 1024 + 1024]
                box = 4 * cx + 2 * cy + cz
                out[box] = (own[box] + spread + added).astype(BF)


def finish(*operands):
    return call(
        final_kernel,
        jax.ShapeDtypeStruct((8, 32, 1024), BF),
        [pltpu.VMEM((512, 128), BF), pltpu.VMEM((128, 1024), BF), pltpu.VMEM((64, 2048), BF)],
    )(*operands)


def shift(block, distance):
    count = lax.axis_size("box")
    return lax.ppermute(block, "box", [(i, (i + distance) % count) for i in range(count)])


def crosses(p, step):
    return (p % 2 == 1) if step == 1 else (p % 2 == 0)


def shift_z(block, step):
    boxes, groups = lax.axis_size("box"), lax.axis_size("term")
    route = []
    for p in range(boxes):
        for t in range(groups):
            to = groups - 1 - t if crosses(p, step) else t
            route.append((p * groups + t, ((p + step) % boxes) * groups + to))
    return lax.ppermute(block, ("box", "term"), route)


def z_layer(fine_coeffs, step, p, t):
    other = lax.axis_size("term") - 1 - t
    cross = (p % 2 == 1) if step == 1 else (p % 2 == 0)
    chosen = lax.dynamic_index_in_dim(fine_coeffs, jnp.where(cross, other, t), 0, False)
    layer = chosen.reshape(4, 2, 32, 1024)[:, 1 if step == 1 else 0]
    return shift_z(layer, step)


def steps(fine_coeffs, fine_blocks, coarse_blocks, two_scale, term_exponent):
    p = lax.axis_index("box")
    t = lax.axis_index("term")
    zm = z_layer(fine_coeffs, 1, p, t)
    zp = z_layer(fine_coeffs, -1, p, t)
    own = lax.dynamic_index_in_dim(fine_coeffs, t, 0, False)
    xm_own = shift(own[4:], 16)
    xp_own = shift(own[:4], -16)

    par, fz, ky, st2 = parents_of(own, two_scale)
    czm = shift(par, 1)
    czp = shift(par, -1)

    far_up = jnp.concatenate([zm[2:], zp[2:], par[None], czm[None], czp[None]], axis=0)
    far_dn = jnp.concatenate([zm[:2], zp[:2], par[None], czm[None], czp[None]], axis=0)
    xm_far = shift(far_up, 16)
    xp_far = shift(far_dn, -16)

    made = weights(term_exponent, fine_blocks, coarse_blocks)
    out, send_up, send_dn, out_c = passes(own, zm, zp, xm_own, xp_own, xm_far, xp_far, par, czm, czp, *made)
    low = shift(send_up, 4)
    high = shift(send_dn, -4)
    total = finish(out, out_c, low, high, fz, ky, st2)
    groups = lax.axis_size("term")
    mine = lax.all_to_all(total.reshape(groups, 2, 32, 1024), "term", 0, 0)
    return mine.astype(F32)


def solution(mesh):
    placed = (P(None, "box", None, None), P(), P(), P(), P())
    return jax.shard_map(
        steps,
        mesh=mesh,
        in_specs=placed,
        out_specs=P(None, ("box", "term"), None, None),
        check_vma=False,
    )
```

```python
import jax
import jax.numpy as jnp
from jax import lax
from jax.experimental import pallas as pl
from jax.experimental.pallas import tpu as pltpu
from jax.sharding import PartitionSpec as P


BF = jnp.bfloat16
F32 = jnp.float32
INTERPRET = False
PARAMS = dict(compiler_params=pltpu.CompilerParams(vmem_limit_bytes=40 * 1024 * 1024))


def dot(a, b):
    return jnp.dot(a, b, preferred_element_type=F32)


def dot_t(a, b):
    return lax.dot_general(a, b, (((1,), (1,)), ((), ())), preferred_element_type=F32)


def split(value):
    hi = value.astype(BF)
    return hi, (value - hi.astype(F32)).astype(BF)


def call(kernel, outs, scratch=()):
    return pl.pallas_call(kernel, out_shape=outs, scratch_shapes=list(scratch), interpret=INTERPRET, **PARAMS)


def same(rows, columns, test):
    i = lax.broadcasted_iota(jnp.int32, (rows, columns), 0)
    j = lax.broadcasted_iota(jnp.int32, (rows, columns), 1)
    return test(i, j).astype(F32).astype(BF)


def weight_kernel(
    exponents, fine, coarse,
    wz, wx, my, cwz, cwx, cmy,
    dense, turned, tall, dense_c, turned_c, tall_c,
):
    wz[...] = jnp.zeros(wz.shape, BF)
    cwz[...] = jnp.zeros(cwz.shape, BF)
    dense[...] = jnp.zeros(dense.shape, F32)
    turned[...] = jnp.zeros(turned.shape, F32)
    eye = same(128, 128, lambda i, j: i == j)
    by_parity = same(64, 64, lambda i, j: j == 2 * (i % 32) + i // 32)
    by_four = same(32, 32, lambda i, j: j == 4 * (i % 8) + i // 8)

    def term(t, carry):
        e = exponents[t]
        for d in range(3):
            block = fine[e, d]
            for child in range(2):
                source = d + child
                for y in range(4):
                    row, column = source * 128 + y * 32, y * 64 + child * 32
                    wz[t, row : row + 32, column : column + 32] = block
                wide_block = block.astype(F32)
                dense[source * 32 : source * 32 + 32, child * 32 : child * 32 + 32] = wide_block
                target = 2 + child - d
                turned[child * 32 : child * 32 + 32, target * 32 : target * 32 + 32] = wide_block
        wx[t] = dot_t(eye[:64, :64], dense[...].astype(BF)).astype(BF)
        chosen = dot(by_parity, turned[...].astype(BF))
        for parity in range(2):
            tall[parity, pl.ds(t * 32, 32), :] = chosen[parity * 32 : parity * 32 + 32]
        for d in range(3):
            block = coarse[e, d]
            dense_c[d * 32 : d * 32 + 32, :] = block.astype(F32)
            turned_c[:, (2 - d) * 32 : (2 - d) * 32 + 32] = block.astype(F32)
            for y in range(4):
                cwz[t, d * 128 + y * 32 : d * 128 + y * 32 + 32, y * 32 : y * 32 + 32] = block
        cwx[t] = dot_t(eye[:32, :32], dense_c[...].astype(BF)).astype(BF)
        chosen = dot(by_four, turned_c[...].astype(BF))
        for parity in range(4):
            tall_c[parity, pl.ds(t * 8, 8), :] = chosen[parity * 8 : parity * 8 + 8]
        return carry

    lax.fori_loop(0, 8, term, 0)
    for parity in range(2):
        my[parity * 128 : parity * 128 + 128, :] = dot_t(eye, tall[parity].astype(BF)).astype(BF)
    for parity in range(4):
        cmy[parity * 96 : parity * 96 + 96, :] = dot_t(eye[:96, :96], tall_c[parity].astype(BF)).astype(BF)


def weights(exponents, fine, coarse):
    whole = pl.BlockSpec(memory_space=pltpu.VMEM)
    return pl.pallas_call(
        weight_kernel,
        out_shape=(
            jax.ShapeDtypeStruct((8, 512, 256), BF),
            jax.ShapeDtypeStruct((8, 64, 128), BF),
            jax.ShapeDtypeStruct((256, 256), BF),
            jax.ShapeDtypeStruct((8, 384, 128), BF),
            jax.ShapeDtypeStruct((8, 32, 96), BF),
            jax.ShapeDtypeStruct((384, 64), BF),
        ),
        in_specs=[pl.BlockSpec(memory_space=pltpu.SMEM), whole, whole],
        scratch_shapes=[
            pltpu.VMEM((128, 64), F32),
            pltpu.VMEM((64, 128), F32),
            pltpu.VMEM((2, 256, 128), F32),
            pltpu.VMEM((96, 32), F32),
            pltpu.VMEM((32, 96), F32),
            pltpu.VMEM((4, 64, 96), F32),
        ],
        interpret=INTERPRET,
        name="weights",
        **PARAMS,
    )(exponents, fine, coarse)


def parent_kernel(own, s, out, fz, ky, st2, rows, wide):
    scale = s[...]
    tiled = lax.dot_general(
        scale, same(32, 128, lambda i, j: j % 32 == i), (((0,), (0,)), ((), ())), preferred_element_type=F32
    )
    block = same(128, 128, lambda i, j: i // 32 == j // 32).astype(F32)
    for cz in range(2):
        part = tiled[cz * 32 : cz * 32 + 32]
        fz[cz * 128 : cz * 128 + 128, :] = (jnp.concatenate([part] * 4, axis=0) * block).astype(BF)
    st2[...] = lax.dot_general(
        scale, same(32, 64, lambda i, j: j % 32 == i), (((0,), (0,)), ((), ())), preferred_element_type=F32
    ).astype(BF)
    spread = lax.dot_general(
        scale, same(32, 1024, lambda i, j: j // 32 == i), (((0,), (0,)), ((), ())), preferred_element_type=F32
    )
    lane = lax.broadcasted_iota(jnp.int32, (32, 1024), 1) % 32 == lax.broadcasted_iota(jnp.int32, (32, 1024), 0)
    for y in range(64):
        ky[y * 32 : y * 32 + 32, :] = jnp.where(
            lane, jnp.broadcast_to(spread[y : y + 1], (32, 1024)), 0.0
        ).astype(BF)
    for yg in range(16):
        cy, g = divmod(yg, 8)
        for cx in range(2):
            for cz in range(2):
                rows[yg * 64 + cx * 32 : yg * 64 + cx * 32 + 32, cz * 128 : cz * 128 + 128] = own[
                    4 * cx + 2 * cy + cz, :, g * 128 : g * 128 + 128
                ]
    along_z = dot(rows[...], fz[...]).astype(BF)
    for yg in range(16):
        wide[:, yg * 128 : yg * 128 + 128] = along_z[yg * 64 : yg * 64 + 64]
    along_y = dot(wide[...], ky[...]).astype(BF)
    out[...] = dot(scale, along_y).astype(BF)


def parents_of(own, s):
    return call(
        parent_kernel,
        (
            jax.ShapeDtypeStruct((32, 1024), BF),
            jax.ShapeDtypeStruct((256, 128), BF),
            jax.ShapeDtypeStruct((2048, 1024), BF),
            jax.ShapeDtypeStruct((64, 64), BF),
        ),
        [pltpu.VMEM((1024, 256), BF), pltpu.VMEM((64, 2048), BF)],
    )(own, s)


PITCH_U = 68
PITCH_V = 132
PITCH_CU = 36
PITCH_CV = 100


def fine_kernel(
    own, zm, zp, xm_own, xp_own, xm_far, xp_far, wz, wx, my,
    out, send_up, send_dn,
    left, mid, wide, done,
):
    for cy in range(2):
        sources = [
            [xm_far[cy], xm_own[2 * cy], xm_own[2 * cy + 1], xm_far[2 + cy]],
            [zm[cy], own[2 * cy], own[2 * cy + 1], zp[cy]],
            [zm[2 + cy], own[4 + 2 * cy], own[5 + 2 * cy], zp[2 + cy]],
            [xp_far[cy], xp_own[2 * cy], xp_own[2 * cy + 1], xp_far[2 + cy]],
        ]
        for xb in range(4):
            for zb in range(4):
                box = sources[xb][zb]
                for g in range(8):
                    row = (cy * 8 + g) * 128 + xb * 32
                    left[row : row + 32, zb * 128 : zb * 128 + 128] = box[:, g * 128 : g * 128 + 128]

    def term(t, carry):
        weight = wz[t]
        for m in range(4):
            passed = dot(left[m * 512 : m * 512 + 512, :], weight).astype(BF)
            mid[m * 4 : m * 4 + 4] = passed.reshape(4, 128, 256)
        weight_x = wx[t]
        start = pl.multiple_of(t * (32 * PITCH_U), 8)
        for yg in range(16):
            passed = dot(weight_x, mid[yg])
            wide[pl.ds(start + 2 * yg * PITCH_U, 64), :] = passed[:, :128]
            wide[pl.ds(start + (2 * yg + 1) * PITCH_U, 64), :] = passed[:, 128:]
        return carry

    lax.fori_loop(0, 8, term, 0)

    def rows(k, carry):
        u = 2 * k
        data = jnp.concatenate(
            [wide[pl.ds(u + i, 256, stride=PITCH_U), :].astype(BF) for i in range(2)], axis=1
        )
        passed = dot(my[...], data)
        start = pl.multiple_of(k * (2 * PITCH_V), 8)
        for i in range(2):
            lanes = passed[:, i * 128 : i * 128 + 128]
            done[pl.ds(start + i * PITCH_V, 128), :] = lanes[:128] + pltpu.roll(lanes[128:], 64, 1)
        return carry

    lax.fori_loop(0, 32, rows, 0)

    lane = lax.broadcasted_iota(jnp.int32, (64, 128), 1) // 32

    def relay(g, carry):
        at = pl.multiple_of(g * 128, 128)
        for vb in range(4):
            parts = [done[pl.ds(vb * 32 + 4 * g + j, 64, stride=PITCH_V), :] for j in range(4)]
            for cz in range(2):
                block = parts[0] if cz == 0 else pltpu.roll(parts[0], 96, 1)
                for j in range(1, 4):
                    turn = (32 * (j - cz)) % 128
                    moved = pltpu.roll(parts[j], turn, 1) if turn else parts[j]
                    block = jnp.where(lane == j, moved, block)
                for cx in range(2):
                    piece = block[cx * 32 : cx * 32 + 32]
                    if vb == 0:
                        send_dn[2 * cx + cz, :, pl.ds(at, 128)] = piece.astype(BF)
                    elif vb == 3:
                        send_up[2 * cx + cz, :, pl.ds(at, 128)] = piece.astype(BF)
                    else:
                        out[4 * cx + 2 * (vb - 1) + cz, :, pl.ds(at, 128)] = piece
        return carry

    lax.fori_loop(0, 8, relay, 0)


def fine_passes(*operands):
    return call(
        fine_kernel,
        (
            jax.ShapeDtypeStruct((8, 32, 1024), F32),
            jax.ShapeDtypeStruct((4, 32, 1024), BF),
            jax.ShapeDtypeStruct((4, 32, 1024), BF),
        ),
        [
            pltpu.VMEM((2048, 512), BF),
            pltpu.VMEM((16, 128, 256), BF),
            pltpu.VMEM((256 * PITCH_U, 128), F32),
            pltpu.VMEM((64 * PITCH_V, 128), F32),
        ],
    )(*operands)


def coarse_kernel(par, zm, zp, xm, xp, wz, wx, my, out, send_up, send_dn, left, mid, wide, done):
    sources = [
        [xm[1], xm[0], xm[2]],
        [zm[...], par[...], zp[...]],
        [xp[1], xp[0], xp[2]],
    ]
    for xb in range(3):
        for zb in range(3):
            for g in range(8):
                row = g * 96 + xb * 32
                left[row : row + 32, zb * 128 : zb * 128 + 128] = sources[xb][zb][:, g * 128 : g * 128 + 128]

    def pair(h, carry):
        weight = jnp.concatenate([wz[2 * h], wz[2 * h + 1]], axis=1)
        mid[...] = dot(left[...], weight).astype(BF).reshape(8, 96, 256)
        start = pl.multiple_of(h * (16 * PITCH_CU), 8)
        for i in range(2):
            weight_x = wx[2 * h + i]
            for g in range(0, 8, 2):
                data = jnp.concatenate(
                    [mid[g, :, i * 128 : i * 128 + 128], mid[g + 1, :, i * 128 : i * 128 + 128]], axis=1
                )
                moved = dot(weight_x, data)
                wide[pl.ds(start + (i * 8 + g) * PITCH_CU, 32), :] = moved[:, :128]
                wide[pl.ds(start + (i * 8 + g + 1) * PITCH_CU, 32), :] = moved[:, 128:]
        return carry

    lax.fori_loop(0, 4, pair, 0)

    def rows(k, carry):
        u = 2 * k
        data = jnp.concatenate(
            [wide[pl.ds(u + i, 64, stride=PITCH_CU), :].astype(BF) for i in range(2)], axis=1
        )
        passed = dot(my[...], data)
        start = pl.multiple_of(k * (2 * PITCH_CV), 8)
        for i in range(2):
            lanes = passed[:, i * 128 : i * 128 + 128]
            total = lanes[:96]
            for j in range(1, 4):
                total = total + pltpu.roll(lanes[j * 96 : j * 96 + 96], 128 - 32 * j, 1)
            done[pl.ds(start + i * PITCH_CV, 96), :] = total
        return carry

    lax.fori_loop(0, 16, rows, 0)

    lane = lax.broadcasted_iota(jnp.int32, (32, 128), 1) // 32

    def relay(g, carry):
        at = pl.multiple_of(g * 128, 128)
        for vb in range(3):
            block = done[pl.ds(vb * 32 + 4 * g, 32, stride=PITCH_CV), :]
            for j in range(1, 4):
                part = done[pl.ds(vb * 32 + 4 * g + j, 32, stride=PITCH_CV), :]
                block = jnp.where(lane == j, pltpu.roll(part, 32 * j, 1), block)
            if vb == 0:
                send_dn[:, pl.ds(at, 128)] = block.astype(BF)
            elif vb == 2:
                send_up[:, pl.ds(at, 128)] = block.astype(BF)
            else:
                out[:, pl.ds(at, 128)] = block
        return carry

    lax.fori_loop(0, 8, relay, 0)


def coarse_passes(*operands):
    return call(
        coarse_kernel,
        (
            jax.ShapeDtypeStruct((32, 1024), F32),
            jax.ShapeDtypeStruct((32, 1024), BF),
            jax.ShapeDtypeStruct((32, 1024), BF),
        ),
        [
            pltpu.VMEM((768, 384), BF),
            pltpu.VMEM((8, 96, 256), BF),
            pltpu.VMEM((64 * PITCH_CU, 128), F32),
            pltpu.VMEM((32 * PITCH_CV, 128), F32),
        ],
    )(*operands)


def final_kernel(own, own_c, low, high, low_c, high_c, fz, ky, st2, out, rows, mixed, deep):
    total = own_c[...] + low_c[...].astype(F32) + high_c[...].astype(F32)
    hi, lo = split(total)
    for g in range(8):
        rows[g * 64 : g * 64 + 32, :] = hi[:, g * 128 : g * 128 + 128]
        rows[g * 64 + 32 : g * 64 + 64, :] = lo[:, g * 128 : g * 128 + 128]
    along_z = dot_t(rows[...], fz[...])
    for g in range(8):
        both = along_z[g * 64 : g * 64 + 32] + along_z[g * 64 + 32 : g * 64 + 64]
        hi, lo = split(both)
        for cz in range(2):
            mixed[cz * 64 : cz * 64 + 32, g * 128 : g * 128 + 128] = hi[:, cz * 128 : cz * 128 + 128]
            mixed[cz * 64 + 32 : cz * 64 + 64, g * 128 : g * 128 + 128] = lo[:, cz * 128 : cz * 128 + 128]
    along_y = dot_t(mixed[...], ky[...])
    for cz in range(2):
        hi, lo = split(along_y[cz * 64 : cz * 64 + 32] + along_y[cz * 64 + 32 : cz * 64 + 64])
        deep[:32, :] = hi
        deep[32:, :] = lo
        along_x = dot(st2[...], deep[...])
        for cx in range(2):
            for cy in range(2):
                added = (low if cy == 0 else high)[2 * cx + cz].astype(F32)
                spread = along_x[cx * 32 : cx * 32 + 32, cy * 1024 : cy * 1024 + 1024]
                box = 4 * cx + 2 * cy + cz
                out[box] = (own[box] + spread + added).astype(BF)


def finish(*operands):
    return call(
        final_kernel,
        jax.ShapeDtypeStruct((8, 32, 1024), BF),
        [pltpu.VMEM((512, 128), BF), pltpu.VMEM((128, 1024), BF), pltpu.VMEM((64, 2048), BF)],
    )(*operands)


def shift(block, distance):
    count = lax.axis_size("box")
    return lax.ppermute(block, "box", [(i, (i + distance) % count) for i in range(count)])


def crosses(p, step):
    return (p % 2 == 1) if step == 1 else (p % 2 == 0)


def shift_z(block, step):
    boxes, groups = lax.axis_size("box"), lax.axis_size("term")
    route = []
    for p in range(boxes):
        for t in range(groups):
            to = groups - 1 - t if crosses(p, step) else t
            route.append((p * groups + t, ((p + step) % boxes) * groups + to))
    return lax.ppermute(block, ("box", "term"), route)


def z_layer(fine_coeffs, step, p, t):
    other = lax.axis_size("term") - 1 - t
    cross = (p % 2 == 1) if step == 1 else (p % 2 == 0)
    chosen = lax.dynamic_index_in_dim(fine_coeffs, jnp.where(cross, other, t), 0, False)
    layer = chosen.reshape(4, 2, 32, 1024)[:, 1 if step == 1 else 0]
    return shift_z(layer, step)


def steps(fine_coeffs, fine_blocks, coarse_blocks, two_scale, term_exponent):
    p = lax.axis_index("box")
    t = lax.axis_index("term")
    zm = z_layer(fine_coeffs, 1, p, t)
    zp = z_layer(fine_coeffs, -1, p, t)
    own = lax.dynamic_index_in_dim(fine_coeffs, t, 0, False)
    xm_own = shift(own[4:], 16)
    xp_own = shift(own[:4], -16)

    par, fz, ky, st2 = parents_of(own, two_scale)
    czm = shift(par, 1)
    czp = shift(par, -1)

    xm_far = shift(jnp.concatenate([zm[2:], zp[2:]], axis=0), 16)
    xp_far = shift(jnp.concatenate([zm[:2], zp[:2]], axis=0), -16)
    wz, wx, my, cwz, cwx, cmy = weights(term_exponent, fine_blocks, coarse_blocks)
    planes = jnp.stack([par, czm, czp])
    cxm = shift(planes, 16)
    cxp = shift(planes, -16)

    out, send_up, send_dn = fine_passes(own, zm, zp, xm_own, xp_own, xm_far, xp_far, wz, wx, my)
    low = shift(send_up, 4)
    high = shift(send_dn, -4)
    out_c, send_up_c, send_dn_c = coarse_passes(par, czm, czp, cxm, cxp, cwz, cwx, cmy)
    low_c = shift(send_up_c, 4)
    high_c = shift(send_dn_c, -4)
    total = finish(out, out_c, low, high, low_c, high_c, fz, ky, st2)
    groups = lax.axis_size("term")
    mine = lax.all_to_all(total.reshape(groups, 2, 32, 1024), "term", 0, 0)
    return mine.astype(F32)


def solution(mesh):
    placed = (P(None, "box", None, None), P(), P(), P(), P())
    return jax.shard_map(
        steps,
        mesh=mesh,
        in_specs=placed,
        out_specs=P(None, ("box", "term"), None, None),
        check_vma=False,
    )
```

```python
import jax
import jax.numpy as jnp
from jax import lax
from jax.experimental import pallas as pl
from jax.experimental.pallas import tpu as pltpu
from jax.sharding import PartitionSpec as P


BF = jnp.bfloat16
F32 = jnp.float32
INTERPRET = False
PARAMS = dict(compiler_params=pltpu.CompilerParams(vmem_limit_bytes=40 * 1024 * 1024))


def dot(a, b):
    return jnp.dot(a, b, preferred_element_type=F32)


def dot_t(a, b):
    return lax.dot_general(a, b, (((1,), (1,)), ((), ())), preferred_element_type=F32)


def split(value):
    hi = value.astype(BF)
    return hi, (value - hi.astype(F32)).astype(BF)


def call(kernel, outs, scratch=()):
    return pl.pallas_call(kernel, out_shape=outs, scratch_shapes=list(scratch), interpret=INTERPRET, **PARAMS)


def same(rows, columns, test):
    i = lax.broadcasted_iota(jnp.int32, (rows, columns), 0)
    j = lax.broadcasted_iota(jnp.int32, (rows, columns), 1)
    return test(i, j).astype(F32).astype(BF)


def weight_kernel(
    exponents, fine, coarse,
    wz, wx, my, cwz, cwx, cmy,
    dense, turned, tall, dense_c, turned_c, tall_c,
):
    wz[...] = jnp.zeros(wz.shape, BF)
    cwz[...] = jnp.zeros(cwz.shape, BF)
    dense[...] = jnp.zeros(dense.shape, F32)
    turned[...] = jnp.zeros(turned.shape, F32)
    eye = same(128, 128, lambda i, j: i == j)
    by_parity = same(64, 64, lambda i, j: j == 2 * (i % 32) + i // 32)
    by_four = same(32, 32, lambda i, j: j == 4 * (i % 8) + i // 8)

    def term(t, carry):
        e = exponents[t]
        for d in range(3):
            block = fine[e, d]
            for child in range(2):
                source = d + child
                for y in range(4):
                    row, column = source * 128 + y * 32, y * 64 + child * 32
                    wz[t, row : row + 32, column : column + 32] = block
                wide_block = block.astype(F32)
                dense[source * 32 : source * 32 + 32, child * 32 : child * 32 + 32] = wide_block
                target = 2 + child - d
                turned[child * 32 : child * 32 + 32, target * 32 : target * 32 + 32] = wide_block
        wx[t] = dot_t(eye[:64, :64], dense[...].astype(BF)).astype(BF)
        chosen = dot(by_parity, turned[...].astype(BF))
        for parity in range(2):
            tall[parity, pl.ds(t * 32, 32), :] = chosen[parity * 32 : parity * 32 + 32]
        for d in range(3):
            block = coarse[e, d]
            dense_c[d * 32 : d * 32 + 32, :] = block.astype(F32)
            turned_c[:, (2 - d) * 32 : (2 - d) * 32 + 32] = block.astype(F32)
            for y in range(4):
                cwz[t, d * 128 + y * 32 : d * 128 + y * 32 + 32, y * 32 : y * 32 + 32] = block
        cwx[t] = dot_t(eye[:32, :32], dense_c[...].astype(BF)).astype(BF)
        chosen = dot(by_four, turned_c[...].astype(BF))
        for parity in range(4):
            tall_c[parity, pl.ds(t * 8, 8), :] = chosen[parity * 8 : parity * 8 + 8]
        return carry

    lax.fori_loop(0, 8, term, 0)
    for parity in range(2):
        moved = dot_t(eye, tall[parity].astype(BF)).astype(BF)
        my[0, parity * 64 : parity * 64 + 32, :] = moved[:32]
        my[0, parity * 64 + 32 : parity * 64 + 64, :] = moved[96:]
        my[1, parity * 64 : parity * 64 + 64, :] = moved[32:96]
    for parity in range(4):
        cmy[parity * 96 : parity * 96 + 96, :] = dot_t(eye[:96, :96], tall_c[parity].astype(BF)).astype(BF)


def weights(exponents, fine, coarse):
    whole = pl.BlockSpec(memory_space=pltpu.VMEM)
    return pl.pallas_call(
        weight_kernel,
        out_shape=(
            jax.ShapeDtypeStruct((8, 512, 256), BF),
            jax.ShapeDtypeStruct((8, 64, 128), BF),
            jax.ShapeDtypeStruct((2, 128, 256), BF),
            jax.ShapeDtypeStruct((8, 384, 128), BF),
            jax.ShapeDtypeStruct((8, 32, 96), BF),
            jax.ShapeDtypeStruct((384, 64), BF),
        ),
        in_specs=[pl.BlockSpec(memory_space=pltpu.SMEM), whole, whole],
        scratch_shapes=[
            pltpu.VMEM((128, 64), F32),
            pltpu.VMEM((64, 128), F32),
            pltpu.VMEM((2, 256, 128), F32),
            pltpu.VMEM((96, 32), F32),
            pltpu.VMEM((32, 96), F32),
            pltpu.VMEM((4, 64, 96), F32),
        ],
        interpret=INTERPRET,
        name="weights",
        **PARAMS,
    )(exponents, fine, coarse)


def parent_kernel(where, boxes, s, out, up, dn, fz, ky, st2, rows, wide):
    step = pl.program_id(0)
    scale = s[...]

    @pl.when(step == 0)
    def _():
        tiled = lax.dot_general(
            scale, same(32, 128, lambda i, j: j % 32 == i), (((0,), (0,)), ((), ())), preferred_element_type=F32
        )
        block = same(128, 128, lambda i, j: i // 32 == j // 32).astype(F32)
        for cz in range(2):
            part = tiled[cz * 32 : cz * 32 + 32]
            fz[cz * 128 : cz * 128 + 128, :] = (jnp.concatenate([part] * 4, axis=0) * block).astype(BF)
        st2[...] = lax.dot_general(
            scale, same(32, 64, lambda i, j: j % 32 == i), (((0,), (0,)), ((), ())), preferred_element_type=F32
        ).astype(BF)
        spread = lax.dot_general(
            scale, same(32, 1024, lambda i, j: j // 32 == i), (((0,), (0,)), ((), ())), preferred_element_type=F32
        )
        lane = lax.broadcasted_iota(jnp.int32, (32, 1024), 1) % 32 == lax.broadcasted_iota(jnp.int32, (32, 1024), 0)
        for y in range(64):
            ky[y * 32 : y * 32 + 32, :] = jnp.where(
                lane, jnp.broadcast_to(spread[y : y + 1], (32, 1024)), 0.0
            ).astype(BF)

    for yg in range(16):
        cy, g = divmod(yg, 8)
        for cx in range(2):
            for cz in range(2):
                rows[yg * 64 + cx * 32 : yg * 64 + cx * 32 + 32, cz * 128 : cz * 128 + 128] = boxes[
                    0, 4 * cx + 2 * cy + cz, :, g * 128 : g * 128 + 128
                ]
    along_z = dot(rows[...], fz[...]).astype(BF)
    for yg in range(16):
        wide[:, yg * 128 : yg * 128 + 128] = along_z[yg * 64 : yg * 64 + 64]
    along_y = dot(wide[...], ky[...]).astype(BF)
    parent = dot(scale, along_y).astype(BF)

    @pl.when(step == 0)
    def _():
        out[...] = parent

    @pl.when(step == where[2])
    def _():
        up[...] = parent

    @pl.when(step != where[2])
    def _():
        dn[...] = parent


def parents_of(where, fine_coeffs, s):
    def whole(*shape):
        return pl.BlockSpec(shape, lambda i, w: (0,) * len(shape))

    return pl.pallas_call(
        parent_kernel,
        out_shape=(
            jax.ShapeDtypeStruct((32, 1024), BF),
            jax.ShapeDtypeStruct((32, 1024), BF),
            jax.ShapeDtypeStruct((32, 1024), BF),
            jax.ShapeDtypeStruct((256, 128), BF),
            jax.ShapeDtypeStruct((2048, 1024), BF),
            jax.ShapeDtypeStruct((64, 64), BF),
        ),
        grid_spec=pltpu.PrefetchScalarGridSpec(
            num_scalar_prefetch=1,
            grid=(2,),
            in_specs=[pl.BlockSpec((1, 8, 32, 1024), lambda i, w: (w[i], 0, 0, 0)), whole(32, 64)],
            out_specs=[
                whole(32, 1024), whole(32, 1024), whole(32, 1024), whole(256, 128), whole(2048, 1024), whole(64, 64),
            ],
            scratch_shapes=[pltpu.VMEM((1024, 256), BF), pltpu.VMEM((64, 2048), BF)],
        ),
        interpret=INTERPRET,
        name="parents",
        **PARAMS,
    )(where, fine_coeffs, s)


PITCH_U = 68
PITCH_CU = 36
PITCH_CV = 100


def fill_left(left, sources, row):
    for zb in range(4):
        for g in range(8):
            left[row + g * 64 : row + g * 64 + 32, zb * 128 : zb * 128 + 128] = sources[zb][:, g * 128 : g * 128 + 128]


def inner_kernel(own, zm, zp, wz, mid, left):
    for cy in range(2):
        for cx in range(2):
            at = 4 * cx + 2 * cy
            fill_left(left, [zm[2 * cx + cy], own[at], own[at + 1], zp[2 * cx + cy]], cy * 512 + cx * 32)

    def term(t, carry):
        weight = wz[t]
        for m in range(2):
            passed = dot(left[m * 512 : m * 512 + 512, :], weight).astype(BF)
            mid[t, m * 8 : m * 8 + 8] = passed.reshape(8, 64, 256)
        return carry

    lax.fori_loop(0, 8, term, 0)


def inner_pass(*operands):
    return call(inner_kernel, jax.ShapeDtypeStruct((8, 16, 64, 256), BF), [pltpu.VMEM((1024, 512), BF)])(*operands)


def fold_rows(passed, done, start, pitch):
    for i in range(4):
        lanes = passed[:, i * 128 : i * 128 + 128]
        done[pl.ds(start + i * pitch, 64), :] = lanes[:64] + pltpu.roll(lanes[64:], 64, 1)


def gather_lanes(done, first, g, cz, lane):
    block = None
    for j in range(4):
        part = done[pl.ds(first + 4 * g + j, 64, stride=PITCH_U), :]
        turn = (32 * (j - cz)) % 128
        moved = pltpu.roll(part, turn, 1) if turn else part
        block = moved if block is None else jnp.where(lane == j, moved, block)
    return block


def outer_kernel(
    inner, xm_own, xp_own, xm_far, xp_far, wz, wx, my,
    send_up, send_dn, packed,
    left, mid, wide, done,
):
    for cy in range(2):
        own = 2 * cy
        fill_left(left, [xm_far[cy], xm_own[own], xm_own[own + 1], xm_far[2 + cy]], cy * 512)
        fill_left(left, [xp_far[cy], xp_own[own], xp_own[own + 1], xp_far[2 + cy]], cy * 512 + 32)

    def term(t, carry):
        weight = wz[t]
        for m in range(2):
            passed = dot(left[m * 512 : m * 512 + 512, :], weight).astype(BF)
            mid[m * 8 : m * 8 + 8] = passed.reshape(8, 64, 256)
        weight_x = wx[t]
        start = pl.multiple_of(t * (32 * PITCH_U), 8)
        for yg in range(16):
            data = jnp.concatenate([mid[yg, :32], inner[t, yg], mid[yg, 32:]], axis=0)
            passed = dot(weight_x, data)
            wide[pl.ds(start + 2 * yg * PITCH_U, 64), :] = passed[:, :128]
            wide[pl.ds(start + (2 * yg + 1) * PITCH_U, 64), :] = passed[:, 128:]
        return carry

    lax.fori_loop(0, 8, term, 0)

    def rows(k, carry):
        data = jnp.concatenate(
            [wide[pl.ds(4 * k + i, 256, stride=PITCH_U), :].astype(BF) for i in range(4)], axis=1
        )
        packed[k] = data
        fold_rows(dot(my[0], data), done, pl.multiple_of(k * (4 * PITCH_U), 8), PITCH_U)
        return carry

    lax.fori_loop(0, 16, rows, 0)

    lane = lax.broadcasted_iota(jnp.int32, (64, 128), 1) // 32

    def relay(g, carry):
        at = pl.multiple_of(g * 128, 128)
        for side in range(2):
            target = send_up if side else send_dn
            for cz in range(2):
                block = gather_lanes(done, side * 32, g, cz, lane).astype(BF)
                for cx in range(2):
                    target[2 * cx + cz, :, pl.ds(at, 128)] = block[cx * 32 : cx * 32 + 32]
        return carry

    lax.fori_loop(0, 8, relay, 0)


def outer_passes(*operands):
    return call(
        outer_kernel,
        (
            jax.ShapeDtypeStruct((4, 32, 1024), BF),
            jax.ShapeDtypeStruct((4, 32, 1024), BF),
            jax.ShapeDtypeStruct((16, 256, 512), BF),
        ),
        [
            pltpu.VMEM((1024, 512), BF),
            pltpu.VMEM((16, 64, 256), BF),
            pltpu.VMEM((256 * PITCH_U, 128), F32),
            pltpu.VMEM((64 * PITCH_U, 128), F32),
        ],
    )(*operands)


def own_kernel(packed, my, out, done):
    def rows(k, carry):
        fold_rows(dot(my[1], packed[k]), done, pl.multiple_of(k * (4 * PITCH_U), 8), PITCH_U)
        return carry

    lax.fori_loop(0, 16, rows, 0)

    lane = lax.broadcasted_iota(jnp.int32, (64, 128), 1) // 32

    def relay(g, carry):
        at = pl.multiple_of(g * 128, 128)
        for cy in range(2):
            for cz in range(2):
                block = gather_lanes(done, cy * 32, g, cz, lane)
                for cx in range(2):
                    out[4 * cx + 2 * cy + cz, :, pl.ds(at, 128)] = block[cx * 32 : cx * 32 + 32]
        return carry

    lax.fori_loop(0, 8, relay, 0)


def own_rows(*operands):
    return call(own_kernel, jax.ShapeDtypeStruct((8, 32, 1024), F32), [pltpu.VMEM((64 * PITCH_U, 128), F32)])(*operands)


def coarse_kernel(par, zm, zp, xm, xp, wz, wx, my, out, send_up, send_dn, left, mid, wide, done):
    sources = [
        [xm[1], xm[0], xm[2]],
        [zm[...], par[...], zp[...]],
        [xp[1], xp[0], xp[2]],
    ]
    for xb in range(3):
        for zb in range(3):
            for g in range(8):
                row = g * 96 + xb * 32
                left[row : row + 32, zb * 128 : zb * 128 + 128] = sources[xb][zb][:, g * 128 : g * 128 + 128]

    def pair(h, carry):
        weight = jnp.concatenate([wz[2 * h], wz[2 * h + 1]], axis=1)
        mid[...] = dot(left[...], weight).astype(BF).reshape(8, 96, 256)
        start = pl.multiple_of(h * (16 * PITCH_CU), 8)
        for i in range(2):
            weight_x = wx[2 * h + i]
            for g in range(0, 8, 2):
                data = jnp.concatenate(
                    [mid[g, :, i * 128 : i * 128 + 128], mid[g + 1, :, i * 128 : i * 128 + 128]], axis=1
                )
                moved = dot(weight_x, data)
                wide[pl.ds(start + (i * 8 + g) * PITCH_CU, 32), :] = moved[:, :128]
                wide[pl.ds(start + (i * 8 + g + 1) * PITCH_CU, 32), :] = moved[:, 128:]
        return carry

    lax.fori_loop(0, 4, pair, 0)

    def rows(k, carry):
        data = jnp.concatenate(
            [wide[pl.ds(4 * k + i, 64, stride=PITCH_CU), :].astype(BF) for i in range(4)], axis=1
        )
        passed = dot(my[...], data)
        start = pl.multiple_of(k * (4 * PITCH_CV), 8)
        for i in range(4):
            lanes = passed[:, i * 128 : i * 128 + 128]
            total = lanes[:96]
            for j in range(1, 4):
                total = total + pltpu.roll(lanes[j * 96 : j * 96 + 96], 128 - 32 * j, 1)
            done[pl.ds(start + i * PITCH_CV, 96), :] = total
        return carry

    lax.fori_loop(0, 8, rows, 0)

    lane = lax.broadcasted_iota(jnp.int32, (32, 128), 1) // 32

    def relay(g, carry):
        at = pl.multiple_of(g * 128, 128)
        for vb in range(3):
            block = done[pl.ds(vb * 32 + 4 * g, 32, stride=PITCH_CV), :]
            for j in range(1, 4):
                part = done[pl.ds(vb * 32 + 4 * g + j, 32, stride=PITCH_CV), :]
                block = jnp.where(lane == j, pltpu.roll(part, 32 * j, 1), block)
            if vb == 0:
                send_dn[:, pl.ds(at, 128)] = block.astype(BF)
            elif vb == 2:
                send_up[:, pl.ds(at, 128)] = block.astype(BF)
            else:
                out[:, pl.ds(at, 128)] = block
        return carry

    lax.fori_loop(0, 8, relay, 0)


def coarse_passes(*operands):
    return call(
        coarse_kernel,
        (
            jax.ShapeDtypeStruct((32, 1024), F32),
            jax.ShapeDtypeStruct((32, 1024), BF),
            jax.ShapeDtypeStruct((32, 1024), BF),
        ),
        [
            pltpu.VMEM((768, 384), BF),
            pltpu.VMEM((8, 96, 256), BF),
            pltpu.VMEM((64 * PITCH_CU, 128), F32),
            pltpu.VMEM((32 * PITCH_CV, 128), F32),
        ],
    )(*operands)


def final_kernel(own, own_c, low, high, low_c, high_c, fz, ky, st2, out, rows, mixed, deep):
    total = own_c[...] + low_c[...].astype(F32) + high_c[...].astype(F32)
    hi, lo = split(total)
    for g in range(8):
        rows[g * 64 : g * 64 + 32, :] = hi[:, g * 128 : g * 128 + 128]
        rows[g * 64 + 32 : g * 64 + 64, :] = lo[:, g * 128 : g * 128 + 128]
    along_z = dot_t(rows[...], fz[...])
    for g in range(8):
        both = along_z[g * 64 : g * 64 + 32] + along_z[g * 64 + 32 : g * 64 + 64]
        hi, lo = split(both)
        for cz in range(2):
            mixed[cz * 64 : cz * 64 + 32, g * 128 : g * 128 + 128] = hi[:, cz * 128 : cz * 128 + 128]
            mixed[cz * 64 + 32 : cz * 64 + 64, g * 128 : g * 128 + 128] = lo[:, cz * 128 : cz * 128 + 128]
    along_y = dot_t(mixed[...], ky[...])
    for cz in range(2):
        hi, lo = split(along_y[cz * 64 : cz * 64 + 32] + along_y[cz * 64 + 32 : cz * 64 + 64])
        deep[:32, :] = hi
        deep[32:, :] = lo
        along_x = dot(st2[...], deep[...])
        for cx in range(2):
            for cy in range(2):
                added = (low if cy == 0 else high)[2 * cx + cz].astype(F32)
                spread = along_x[cx * 32 : cx * 32 + 32, cy * 1024 : cy * 1024 + 1024]
                box = 4 * cx + 2 * cy + cz
                out[box] = (own[box] + spread + added).astype(BF)


def finish(*operands):
    return call(
        final_kernel,
        jax.ShapeDtypeStruct((8, 32, 1024), BF),
        [pltpu.VMEM((512, 128), BF), pltpu.VMEM((128, 1024), BF), pltpu.VMEM((64, 2048), BF)],
    )(*operands)


def shift(block, distance):
    count = lax.axis_size("box")
    return lax.ppermute(block, "box", [(i, (i + distance) % count) for i in range(count)])


def crosses(p, step):
    return (p % 2 == 1) if step == 1 else (p % 2 == 0)


def shift_z(block, step):
    boxes, groups = lax.axis_size("box"), lax.axis_size("term")
    route = []
    for p in range(boxes):
        for t in range(groups):
            to = groups - 1 - t if crosses(p, step) else t
            route.append((p * groups + t, ((p + step) % boxes) * groups + to))
    return lax.ppermute(block, ("box", "term"), route)


def z_layer(fine_coeffs, step, p, t):
    other = lax.axis_size("term") - 1 - t
    cross = (p % 2 == 1) if step == 1 else (p % 2 == 0)
    chosen = lax.dynamic_index_in_dim(fine_coeffs, jnp.where(cross, other, t), 0, False)
    layer = chosen.reshape(4, 2, 32, 1024)[:, 1 if step == 1 else 0]
    return shift_z(layer, step)


def steps(fine_coeffs, fine_blocks, coarse_blocks, two_scale, term_exponent):
    p = lax.axis_index("box")
    t = lax.axis_index("term")
    zm = z_layer(fine_coeffs, 1, p, t)
    zp = z_layer(fine_coeffs, -1, p, t)
    own = lax.dynamic_index_in_dim(fine_coeffs, t, 0, False)
    xm_own = shift(own[4:], 16)
    xp_own = shift(own[:4], -16)

    other = lax.axis_size("term") - 1 - t
    where = jnp.stack([t, other, p % 2]).astype(jnp.int32)
    par, par_up, par_dn, fz, ky, st2 = parents_of(where, fine_coeffs, two_scale)
    wz, wx, my, cwz, cwx, cmy = weights(term_exponent, fine_blocks, coarse_blocks)
    xm_far = shift(jnp.concatenate([zm[2:], zp[2:]], axis=0), 16)
    xp_far = shift(jnp.concatenate([zm[:2], zp[:2]], axis=0), -16)
    czm = shift_z(par_up, 1)
    czp = shift_z(par_dn, -1)
    mid = inner_pass(own, zm, zp, wz)
    planes = jnp.stack([par, czm, czp])
    cxm = shift(planes, 16)
    cxp = shift(planes, -16)

    send_up, send_dn, packed = outer_passes(mid, xm_own, xp_own, xm_far, xp_far, wz, wx, my)
    low = shift(send_up, 4)
    high = shift(send_dn, -4)
    out_c, send_up_c, send_dn_c = coarse_passes(par, czm, czp, cxm, cxp, cwz, cwx, cmy)
    low_c = shift(send_up_c, 4)
    high_c = shift(send_dn_c, -4)
    out = own_rows(packed, my)
    total = finish(out, out_c, low, high, low_c, high_c, fz, ky, st2)
    groups = lax.axis_size("term")
    mine = lax.all_to_all(total.reshape(groups, 2, 32, 1024), "term", 0, 0)
    return mine.astype(F32)


def solution(mesh):
    placed = (P(None, "box", None, None), P(), P(), P(), P())
    return jax.shard_map(
        steps,
        mesh=mesh,
        in_specs=placed,
        out_specs=P(None, ("box", "term"), None, None),
        check_vma=False,
    )
```

```python
import jax
import jax.numpy as jnp
from jax import lax
from jax.experimental import pallas as pl
from jax.experimental.pallas import tpu as pltpu
from jax.sharding import PartitionSpec as P


BF = jnp.bfloat16
F32 = jnp.float32
INTERPRET = False


def grant(mebibytes):
    return dict(compiler_params=pltpu.CompilerParams(vmem_limit_bytes=mebibytes * 1024 * 1024))


def dot(a, b):
    return jnp.dot(a, b, preferred_element_type=F32)


def dot_t(a, b):
    return lax.dot_general(a, b, (((1,), (1,)), ((), ())), preferred_element_type=F32)


def split(value):
    hi = value.astype(BF)
    return hi, (value - hi.astype(F32)).astype(BF)


def call(kernel, outs, scratch=(), size=24):
    return pl.pallas_call(kernel, out_shape=outs, scratch_shapes=list(scratch), interpret=INTERPRET, **grant(size))


def same(rows, columns, test):
    i = lax.broadcasted_iota(jnp.int32, (rows, columns), 0)
    j = lax.broadcasted_iota(jnp.int32, (rows, columns), 1)
    return test(i, j).astype(F32).astype(BF)


def weight_kernel(
    exponents, fine, coarse,
    wz, wx, my, cwz, cwx, cmy,
    dense, turned, tall, dense_c, turned_c, tall_c,
):
    wz[...] = jnp.zeros(wz.shape, BF)
    cwz[...] = jnp.zeros(cwz.shape, BF)
    dense[...] = jnp.zeros(dense.shape, F32)
    turned[...] = jnp.zeros(turned.shape, F32)
    eye = same(128, 128, lambda i, j: i == j)
    by_parity = same(64, 64, lambda i, j: j == 2 * (i % 32) + i // 32)
    by_four = same(32, 32, lambda i, j: j == 4 * (i % 8) + i // 8)

    def term(t, carry):
        e = exponents[t]
        for d in range(3):
            block = fine[e, d]
            for child in range(2):
                source = d + child
                for y in range(4):
                    row, column = source * 128 + y * 32, y * 64 + child * 32
                    wz[t, row : row + 32, column : column + 32] = block
                wide_block = block.astype(F32)
                dense[source * 32 : source * 32 + 32, child * 32 : child * 32 + 32] = wide_block
                target = 2 + child - d
                turned[child * 32 : child * 32 + 32, target * 32 : target * 32 + 32] = wide_block
        wx[t] = dot_t(eye[:64, :64], dense[...].astype(BF)).astype(BF)
        chosen = dot(by_parity, turned[...].astype(BF))
        for parity in range(2):
            tall[parity, pl.ds(t * 32, 32), :] = chosen[parity * 32 : parity * 32 + 32]
        for d in range(3):
            block = coarse[e, d]
            dense_c[d * 32 : d * 32 + 32, :] = block.astype(F32)
            turned_c[:, (2 - d) * 32 : (2 - d) * 32 + 32] = block.astype(F32)
            for y in range(4):
                cwz[t, d * 128 + y * 32 : d * 128 + y * 32 + 32, y * 32 : y * 32 + 32] = block
        cwx[t] = dot_t(eye[:32, :32], dense_c[...].astype(BF)).astype(BF)
        chosen = dot(by_four, turned_c[...].astype(BF))
        for parity in range(4):
            tall_c[parity, pl.ds(t * 8, 8), :] = chosen[parity * 8 : parity * 8 + 8]
        return carry

    lax.fori_loop(0, 8, term, 0)
    for parity in range(2):
        moved = dot_t(eye, tall[parity].astype(BF)).astype(BF)
        my[0, parity * 64 : parity * 64 + 32, :] = moved[:32]
        my[0, parity * 64 + 32 : parity * 64 + 64, :] = moved[96:]
        my[1, parity * 64 : parity * 64 + 64, :] = moved[32:96]
    for parity in range(4):
        cmy[parity * 96 : parity * 96 + 96, :] = dot_t(eye[:96, :96], tall_c[parity].astype(BF)).astype(BF)


def weights(exponents, fine, coarse):
    whole = pl.BlockSpec(memory_space=pltpu.VMEM)
    return pl.pallas_call(
        weight_kernel,
        out_shape=(
            jax.ShapeDtypeStruct((8, 512, 256), BF),
            jax.ShapeDtypeStruct((8, 64, 128), BF),
            jax.ShapeDtypeStruct((2, 128, 256), BF),
            jax.ShapeDtypeStruct((8, 384, 128), BF),
            jax.ShapeDtypeStruct((8, 32, 96), BF),
            jax.ShapeDtypeStruct((384, 64), BF),
        ),
        in_specs=[pl.BlockSpec(memory_space=pltpu.SMEM), whole, whole],
        scratch_shapes=[
            pltpu.VMEM((128, 64), F32),
            pltpu.VMEM((64, 128), F32),
            pltpu.VMEM((2, 256, 128), F32),
            pltpu.VMEM((96, 32), F32),
            pltpu.VMEM((32, 96), F32),
            pltpu.VMEM((4, 64, 96), F32),
        ],
        interpret=INTERPRET,
        name="weights",
        **grant(16),
    )(exponents, fine, coarse)


def prepare_kernel(where, boxes, s, out, low_x, high_x, up, dn, fz, ky, st2, rows, wide):
    step = pl.program_id(0)
    scale = s[...]

    @pl.when(step == 0)
    def _():
        tiled = lax.dot_general(
            scale, same(32, 128, lambda i, j: j % 32 == i), (((0,), (0,)), ((), ())), preferred_element_type=F32
        )
        block = same(128, 128, lambda i, j: i // 32 == j // 32).astype(F32)
        for cz in range(2):
            part = tiled[cz * 32 : cz * 32 + 32]
            fz[cz * 128 : cz * 128 + 128, :] = (jnp.concatenate([part] * 4, axis=0) * block).astype(BF)
        st2[...] = lax.dot_general(
            scale, same(32, 64, lambda i, j: j % 32 == i), (((0,), (0,)), ((), ())), preferred_element_type=F32
        ).astype(BF)
        spread = lax.dot_general(
            scale, same(32, 1024, lambda i, j: j // 32 == i), (((0,), (0,)), ((), ())), preferred_element_type=F32
        )
        lane = lax.broadcasted_iota(jnp.int32, (32, 1024), 1) % 32 == lax.broadcasted_iota(jnp.int32, (32, 1024), 0)
        for y in range(64):
            ky[y * 32 : y * 32 + 32, :] = jnp.where(
                lane, jnp.broadcast_to(spread[y : y + 1], (32, 1024)), 0.0
            ).astype(BF)

    for yg in range(16):
        cy, g = divmod(yg, 8)
        for cx in range(2):
            for cz in range(2):
                rows[yg * 64 + cx * 32 : yg * 64 + cx * 32 + 32, cz * 128 : cz * 128 + 128] = boxes[
                    0, 4 * cx + 2 * cy + cz, :, g * 128 : g * 128 + 128
                ]
    along_z = dot(rows[...], fz[...]).astype(BF)
    for yg in range(16):
        wide[:, yg * 128 : yg * 128 + 128] = along_z[yg * 64 : yg * 64 + 64]
    along_y = dot(wide[...], ky[...]).astype(BF)
    parent = dot(scale, along_y).astype(BF)

    @pl.when(step == 0)
    def _():
        out[...] = parent
        low_x[...] = boxes[0, :4]
        high_x[...] = boxes[0, 4:]

    @pl.when(step == where[2])
    def _():
        for i in range(4):
            up[i] = boxes[0, 2 * i + 1]
        up[4] = parent

    @pl.when(step != where[2])
    def _():
        for i in range(4):
            dn[i] = boxes[0, 2 * i]
        dn[4] = parent


def prepare(where, fine_coeffs, s):
    def whole(*shape):
        return pl.BlockSpec(shape, lambda i, w: (0,) * len(shape))

    shapes = [(32, 1024), (4, 32, 1024), (4, 32, 1024), (5, 32, 1024), (5, 32, 1024), (256, 128), (2048, 1024), (64, 64)]
    return pl.pallas_call(
        prepare_kernel,
        out_shape=tuple(jax.ShapeDtypeStruct(shape, BF) for shape in shapes),
        grid_spec=pltpu.PrefetchScalarGridSpec(
            num_scalar_prefetch=1,
            grid=(2,),
            in_specs=[pl.BlockSpec((1, 8, 32, 1024), lambda i, w: (w[i], 0, 0, 0)), whole(32, 64)],
            out_specs=[whole(*shape) for shape in shapes],
            scratch_shapes=[pltpu.VMEM((1024, 256), BF), pltpu.VMEM((64, 2048), BF)],
        ),
        interpret=INTERPRET,
        name="prepare",
        **grant(24),
    )(where, fine_coeffs, s)


PITCH_U = 68
PITCH_CU = 36
PITCH_CV = 100


def fill_left(left, sources, row):
    for zb in range(4):
        for g in range(8):
            left[row + g * 64 : row + g * 64 + 32, zb * 128 : zb * 128 + 128] = sources[zb][:, g * 128 : g * 128 + 128]


def inner_kernel(low_x, high_x, zm, zp, wz, mid, left):
    for cy in range(2):
        for cx in range(2):
            own = high_x if cx else low_x
            fill_left(left, [zm[2 * cx + cy], own[2 * cy], own[2 * cy + 1], zp[2 * cx + cy]], cy * 512 + cx * 32)

    def term(t, carry):
        weight = wz[t]
        for m in range(2):
            passed = dot(left[m * 512 : m * 512 + 512, :], weight).astype(BF)
            mid[t, m * 8 : m * 8 + 8] = passed.reshape(8, 64, 256)
        return carry

    lax.fori_loop(0, 8, term, 0)


def inner_pass(*operands):
    return call(inner_kernel, jax.ShapeDtypeStruct((8, 16, 64, 256), BF), [pltpu.VMEM((1024, 512), BF)])(*operands)


def fold_rows(passed, done, start, pitch):
    for i in range(4):
        lanes = passed[:, i * 128 : i * 128 + 128]
        done[pl.ds(start + i * pitch, 64), :] = lanes[:64] + pltpu.roll(lanes[64:], 64, 1)


def gather_lanes(done, first, g, cz, lane):
    block = None
    for j in range(4):
        part = done[pl.ds(first + 4 * g + j, 64, stride=PITCH_U), :]
        turn = (32 * (j - cz)) % 128
        moved = pltpu.roll(part, turn, 1) if turn else part
        block = moved if block is None else jnp.where(lane == j, moved, block)
    return block


def outer_kernel(
    inner, xm_own, xp_own, xm_far, xp_far, wz, wx, my,
    send_up, send_dn, packed,
    left, mid, wide, done,
):
    for cy in range(2):
        own = 2 * cy
        fill_left(left, [xm_far[cy], xm_own[own], xm_own[own + 1], xm_far[2 + cy]], cy * 512)
        fill_left(left, [xp_far[cy], xp_own[own], xp_own[own + 1], xp_far[2 + cy]], cy * 512 + 32)

    def term(t, carry):
        weight = wz[t]
        for m in range(2):
            passed = dot(left[m * 512 : m * 512 + 512, :], weight).astype(BF)
            mid[m * 8 : m * 8 + 8] = passed.reshape(8, 64, 256)
        weight_x = wx[t]
        start = pl.multiple_of(t * (32 * PITCH_U), 8)
        for yg in range(16):
            data = jnp.concatenate([mid[yg, :32], inner[t, yg], mid[yg, 32:]], axis=0)
            passed = dot(weight_x, data)
            wide[pl.ds(start + 2 * yg * PITCH_U, 64), :] = passed[:, :128]
            wide[pl.ds(start + (2 * yg + 1) * PITCH_U, 64), :] = passed[:, 128:]
        return carry

    lax.fori_loop(0, 8, term, 0)

    def rows(k, carry):
        data = jnp.concatenate(
            [wide[pl.ds(4 * k + i, 256, stride=PITCH_U), :].astype(BF) for i in range(4)], axis=1
        )
        packed[k] = data
        fold_rows(dot(my[0], data), done, pl.multiple_of(k * (4 * PITCH_U), 8), PITCH_U)
        return carry

    lax.fori_loop(0, 16, rows, 0)

    lane = lax.broadcasted_iota(jnp.int32, (64, 128), 1) // 32

    def relay(g, carry):
        at = pl.multiple_of(g * 128, 128)
        for side in range(2):
            target = send_up if side else send_dn
            for cz in range(2):
                block = gather_lanes(done, side * 32, g, cz, lane).astype(BF)
                for cx in range(2):
                    target[2 * cx + cz, :, pl.ds(at, 128)] = block[cx * 32 : cx * 32 + 32]
        return carry

    lax.fori_loop(0, 8, relay, 0)


def outer_passes(*operands):
    return call(
        outer_kernel,
        (
            jax.ShapeDtypeStruct((4, 32, 1024), BF),
            jax.ShapeDtypeStruct((4, 32, 1024), BF),
            jax.ShapeDtypeStruct((16, 256, 512), BF),
        ),
        [
            pltpu.VMEM((1024, 512), BF),
            pltpu.VMEM((16, 64, 256), BF),
            pltpu.VMEM((256 * PITCH_U, 128), F32),
            pltpu.VMEM((64 * PITCH_U, 128), F32),
        ],
    )(*operands)


def own_kernel(packed, my, out, done):
    def rows(k, carry):
        fold_rows(dot(my[1], packed[k]), done, pl.multiple_of(k * (4 * PITCH_U), 8), PITCH_U)
        return carry

    lax.fori_loop(0, 16, rows, 0)

    lane = lax.broadcasted_iota(jnp.int32, (64, 128), 1) // 32

    def relay(g, carry):
        at = pl.multiple_of(g * 128, 128)
        for cy in range(2):
            for cz in range(2):
                block = gather_lanes(done, cy * 32, g, cz, lane)
                for cx in range(2):
                    out[4 * cx + 2 * cy + cz, :, pl.ds(at, 128)] = block[cx * 32 : cx * 32 + 32]
        return carry

    lax.fori_loop(0, 8, relay, 0)


def own_rows(*operands):
    return call(own_kernel, jax.ShapeDtypeStruct((8, 32, 1024), F32), [pltpu.VMEM((64 * PITCH_U, 128), F32)])(*operands)


def coarse_kernel(par, zm, zp, xm, xp, wz, wx, my, out, send_up, send_dn, left, mid, wide, done):
    sources = [
        [xm[1], xm[0], xm[2]],
        [zm[4], par[...], zp[4]],
        [xp[1], xp[0], xp[2]],
    ]
    for xb in range(3):
        for zb in range(3):
            for g in range(8):
                row = g * 96 + xb * 32
                left[row : row + 32, zb * 128 : zb * 128 + 128] = sources[xb][zb][:, g * 128 : g * 128 + 128]

    def pair(h, carry):
        weight = jnp.concatenate([wz[2 * h], wz[2 * h + 1]], axis=1)
        mid[...] = dot(left[...], weight).astype(BF).reshape(8, 96, 256)
        start = pl.multiple_of(h * (16 * PITCH_CU), 8)
        for i in range(2):
            weight_x = wx[2 * h + i]
            for g in range(0, 8, 2):
                data = jnp.concatenate(
                    [mid[g, :, i * 128 : i * 128 + 128], mid[g + 1, :, i * 128 : i * 128 + 128]], axis=1
                )
                moved = dot(weight_x, data)
                wide[pl.ds(start + (i * 8 + g) * PITCH_CU, 32), :] = moved[:, :128]
                wide[pl.ds(start + (i * 8 + g + 1) * PITCH_CU, 32), :] = moved[:, 128:]
        return carry

    lax.fori_loop(0, 4, pair, 0)

    def rows(k, carry):
        data = jnp.concatenate(
            [wide[pl.ds(4 * k + i, 64, stride=PITCH_CU), :].astype(BF) for i in range(4)], axis=1
        )
        passed = dot(my[...], data)
        start = pl.multiple_of(k * (4 * PITCH_CV), 8)
        for i in range(4):
            lanes = passed[:, i * 128 : i * 128 + 128]
            total = lanes[:96]
            for j in range(1, 4):
                total = total + pltpu.roll(lanes[j * 96 : j * 96 + 96], 128 - 32 * j, 1)
            done[pl.ds(start + i * PITCH_CV, 96), :] = total
        return carry

    lax.fori_loop(0, 8, rows, 0)

    lane = lax.broadcasted_iota(jnp.int32, (32, 128), 1) // 32

    def relay(g, carry):
        at = pl.multiple_of(g * 128, 128)
        for vb in range(3):
            block = done[pl.ds(vb * 32 + 4 * g, 32, stride=PITCH_CV), :]
            for j in range(1, 4):
                part = done[pl.ds(vb * 32 + 4 * g + j, 32, stride=PITCH_CV), :]
                block = jnp.where(lane == j, pltpu.roll(part, 32 * j, 1), block)
            if vb == 0:
                send_dn[:, pl.ds(at, 128)] = block.astype(BF)
            elif vb == 2:
                send_up[:, pl.ds(at, 128)] = block.astype(BF)
            else:
                out[:, pl.ds(at, 128)] = block
        return carry

    lax.fori_loop(0, 8, relay, 0)


def coarse_passes(*operands):
    return call(
        coarse_kernel,
        (
            jax.ShapeDtypeStruct((32, 1024), F32),
            jax.ShapeDtypeStruct((32, 1024), BF),
            jax.ShapeDtypeStruct((32, 1024), BF),
        ),
        [
            pltpu.VMEM((768, 384), BF),
            pltpu.VMEM((8, 96, 256), BF),
            pltpu.VMEM((64 * PITCH_CU, 128), F32),
            pltpu.VMEM((32 * PITCH_CV, 128), F32),
        ],
    )(*operands)


def final_kernel(own, own_c, low, high, low_c, high_c, fz, ky, st2, out, rows, mixed, deep):
    total = own_c[...] + low_c[...].astype(F32) + high_c[...].astype(F32)
    hi, lo = split(total)
    for g in range(8):
        rows[g * 64 : g * 64 + 32, :] = hi[:, g * 128 : g * 128 + 128]
        rows[g * 64 + 32 : g * 64 + 64, :] = lo[:, g * 128 : g * 128 + 128]
    along_z = dot_t(rows[...], fz[...])
    for g in range(8):
        both = along_z[g * 64 : g * 64 + 32] + along_z[g * 64 + 32 : g * 64 + 64]
        hi, lo = split(both)
        for cz in range(2):
            mixed[cz * 64 : cz * 64 + 32, g * 128 : g * 128 + 128] = hi[:, cz * 128 : cz * 128 + 128]
            mixed[cz * 64 + 32 : cz * 64 + 64, g * 128 : g * 128 + 128] = lo[:, cz * 128 : cz * 128 + 128]
    along_y = dot_t(mixed[...], ky[...])
    for cz in range(2):
        hi, lo = split(along_y[cz * 64 : cz * 64 + 32] + along_y[cz * 64 + 32 : cz * 64 + 64])
        deep[:32, :] = hi
        deep[32:, :] = lo
        along_x = dot(st2[...], deep[...])
        for cx in range(2):
            for cy in range(2):
                added = (low if cy == 0 else high)[2 * cx + cz].astype(F32)
                spread = along_x[cx * 32 : cx * 32 + 32, cy * 1024 : cy * 1024 + 1024]
                box = 4 * cx + 2 * cy + cz
                out[box] = (own[box] + spread + added).astype(BF)


def finish(*operands):
    return call(
        final_kernel,
        jax.ShapeDtypeStruct((8, 32, 1024), BF),
        [pltpu.VMEM((512, 128), BF), pltpu.VMEM((128, 1024), BF), pltpu.VMEM((64, 2048), BF)],
    )(*operands)


def shift(block, distance):
    count = lax.axis_size("box")
    return lax.ppermute(block, "box", [(i, (i + distance) % count) for i in range(count)])


def crosses(p, step):
    return (p % 2 == 1) if step == 1 else (p % 2 == 0)


def shift_z(block, step):
    boxes, groups = lax.axis_size("box"), lax.axis_size("term")
    route = []
    for p in range(boxes):
        for t in range(groups):
            to = groups - 1 - t if crosses(p, step) else t
            route.append((p * groups + t, ((p + step) % boxes) * groups + to))
    return lax.ppermute(block, ("box", "term"), route)


def steps(fine_coeffs, fine_blocks, coarse_blocks, two_scale, term_exponent):
    p = lax.axis_index("box")
    t = lax.axis_index("term")
    other = lax.axis_size("term") - 1 - t
    where = jnp.stack([t, other, p % 2]).astype(jnp.int32)
    par, low_x, high_x, up, dn, fz, ky, st2 = prepare(where, pltpu.with_memory_space_constraint(fine_coeffs, pltpu.HBM), two_scale)
    zm = shift_z(up, 1)
    zp = shift_z(dn, -1)
    xm_own = shift(high_x, 16)
    xp_own = shift(low_x, -16)
    wz, wx, my, cwz, cwx, cmy = weights(term_exponent, fine_blocks, coarse_blocks)
    xm_far = shift(jnp.concatenate([zm[2:4], zp[2:4]], axis=0), 16)
    xp_far = shift(jnp.concatenate([zm[:2], zp[:2]], axis=0), -16)
    mid = inner_pass(low_x, high_x, zm, zp, wz)
    planes = jnp.stack([par, zm[4], zp[4]])
    cxm = shift(planes, 16)
    cxp = shift(planes, -16)

    send_up, send_dn, packed = outer_passes(mid, xm_own, xp_own, xm_far, xp_far, wz, wx, my)
    low = shift(send_up, 4)
    high = shift(send_dn, -4)
    out_c, send_up_c, send_dn_c = coarse_passes(par, zm, zp, cxm, cxp, cwz, cwx, cmy)
    low_c = shift(send_up_c, 4)
    high_c = shift(send_dn_c, -4)
    out = own_rows(packed, my)
    total = finish(out, out_c, low, high, low_c, high_c, fz, ky, st2)
    groups = lax.axis_size("term")
    mine = lax.all_to_all(total.reshape(groups, 2, 32, 1024), "term", 0, 0)
    return mine.astype(F32)


def solution(mesh):
    placed = (P(None, "box", None, None), P(), P(), P(), P())
    return jax.shard_map(
        steps,
        mesh=mesh,
        in_specs=placed,
        out_specs=P(None, ("box", "term"), None, None),
        check_vma=False,
    )
```

```python
import jax
import jax.numpy as jnp
from jax import lax
from jax.experimental import pallas as pl
from jax.experimental.pallas import tpu as pltpu
from jax.sharding import PartitionSpec as P


BF = jnp.bfloat16
F32 = jnp.float32
INTERPRET = False


def grant(mebibytes):
    return dict(compiler_params=pltpu.CompilerParams(vmem_limit_bytes=mebibytes * 1024 * 1024))


def dot(a, b):
    return jnp.dot(a, b, preferred_element_type=F32)


def dot_t(a, b):
    return lax.dot_general(a, b, (((1,), (1,)), ((), ())), preferred_element_type=F32)


def split(value):
    hi = value.astype(BF)
    return hi, (value - hi.astype(F32)).astype(BF)


def call(kernel, outs, scratch=(), size=24):
    return pl.pallas_call(kernel, out_shape=outs, scratch_shapes=list(scratch), interpret=INTERPRET, **grant(size))


def same(rows, columns, test):
    i = lax.broadcasted_iota(jnp.int32, (rows, columns), 0)
    j = lax.broadcasted_iota(jnp.int32, (rows, columns), 1)
    return test(i, j).astype(F32).astype(BF)


def weight_kernel(
    exponents, fine, coarse,
    wz, wx, my, cwz, cwx, cmy,
    dense, turned, tall, dense_c, turned_c, tall_c,
):
    wz[...] = jnp.zeros(wz.shape, BF)
    cwz[...] = jnp.zeros(cwz.shape, BF)
    dense[...] = jnp.zeros(dense.shape, F32)
    turned[...] = jnp.zeros(turned.shape, F32)
    eye = same(128, 128, lambda i, j: i == j)
    by_parity = same(64, 64, lambda i, j: j == 2 * (i % 32) + i // 32)
    by_four = same(32, 32, lambda i, j: j == 4 * (i % 8) + i // 8)

    def term(t, carry):
        e = exponents[t]
        for d in range(3):
            block = fine[e, d]
            for child in range(2):
                source = d + child
                for y in range(4):
                    row, column = source * 128 + y * 32, y * 64 + child * 32
                    wz[t, row : row + 32, column : column + 32] = block
                wide_block = block.astype(F32)
                dense[source * 32 : source * 32 + 32, child * 32 : child * 32 + 32] = wide_block
                target = 2 + child - d
                turned[child * 32 : child * 32 + 32, target * 32 : target * 32 + 32] = wide_block
        wx[t] = dot_t(eye[:64, :64], dense[...].astype(BF)).astype(BF)
        chosen = dot(by_parity, turned[...].astype(BF))
        for parity in range(2):
            tall[parity, pl.ds(t * 32, 32), :] = chosen[parity * 32 : parity * 32 + 32]
        for d in range(3):
            block = coarse[e, d]
            dense_c[d * 32 : d * 32 + 32, :] = block.astype(F32)
            turned_c[:, (2 - d) * 32 : (2 - d) * 32 + 32] = block.astype(F32)
            for y in range(4):
                cwz[t, d * 128 + y * 32 : d * 128 + y * 32 + 32, y * 32 : y * 32 + 32] = block
        cwx[t] = dot_t(eye[:32, :32], dense_c[...].astype(BF)).astype(BF)
        chosen = dot(by_four, turned_c[...].astype(BF))
        for parity in range(4):
            tall_c[parity, pl.ds(t * 8, 8), :] = chosen[parity * 8 : parity * 8 + 8]
        return carry

    lax.fori_loop(0, 8, term, 0)
    for parity in range(2):
        moved = dot_t(eye, tall[parity].astype(BF)).astype(BF)
        my[0, parity * 64 : parity * 64 + 32, :] = moved[:32]
        my[0, parity * 64 + 32 : parity * 64 + 64, :] = moved[96:]
        my[1, parity * 64 : parity * 64 + 64, :] = moved[32:96]
    for parity in range(4):
        cmy[parity * 96 : parity * 96 + 96, :] = dot_t(eye[:96, :96], tall_c[parity].astype(BF)).astype(BF)


def weights(exponents, fine, coarse):
    whole = pl.BlockSpec(memory_space=pltpu.VMEM)
    return pl.pallas_call(
        weight_kernel,
        out_shape=(
            jax.ShapeDtypeStruct((8, 512, 256), BF),
            jax.ShapeDtypeStruct((8, 64, 128), BF),
            jax.ShapeDtypeStruct((2, 128, 256), BF),
            jax.ShapeDtypeStruct((8, 384, 128), BF),
            jax.ShapeDtypeStruct((8, 32, 96), BF),
            jax.ShapeDtypeStruct((384, 64), BF),
        ),
        in_specs=[pl.BlockSpec(memory_space=pltpu.SMEM), whole, whole],
        scratch_shapes=[
            pltpu.VMEM((128, 64), F32),
            pltpu.VMEM((64, 128), F32),
            pltpu.VMEM((2, 256, 128), F32),
            pltpu.VMEM((96, 32), F32),
            pltpu.VMEM((32, 96), F32),
            pltpu.VMEM((4, 64, 96), F32),
        ],
        interpret=INTERPRET,
        name="weights",
        **grant(16),
    )(exponents, fine, coarse)


def prepare_kernel(where, mine, other, s, out, low_x, high_x, up, dn, fz, ky, st2, rows, wide):
    scale = s[...]
    tiled = lax.dot_general(
        scale, same(32, 128, lambda i, j: j % 32 == i), (((0,), (0,)), ((), ())), preferred_element_type=F32
    )
    block = same(128, 128, lambda i, j: i // 32 == j // 32).astype(F32)
    for cz in range(2):
        part = tiled[cz * 32 : cz * 32 + 32]
        fz[cz * 128 : cz * 128 + 128, :] = (jnp.concatenate([part] * 4, axis=0) * block).astype(BF)
    st2[...] = lax.dot_general(
        scale, same(32, 64, lambda i, j: j % 32 == i), (((0,), (0,)), ((), ())), preferred_element_type=F32
    ).astype(BF)
    spread = lax.dot_general(
        scale, same(32, 1024, lambda i, j: j // 32 == i), (((0,), (0,)), ((), ())), preferred_element_type=F32
    )
    lane = lax.broadcasted_iota(jnp.int32, (32, 1024), 1) % 32 == lax.broadcasted_iota(jnp.int32, (32, 1024), 0)
    for y in range(64):
        ky[y * 32 : y * 32 + 32, :] = jnp.where(
            lane, jnp.broadcast_to(spread[y : y + 1], (32, 1024)), 0.0
        ).astype(BF)
    for yg in range(16):
        cy, g = divmod(yg, 8)
        for k, boxes in enumerate((mine, other)):
            for cx in range(2):
                for cz in range(2):
                    row = yg * 128 + k * 64 + cx * 32
                    rows[row : row + 32, cz * 128 : cz * 128 + 128] = boxes[
                        0, 4 * cx + 2 * cy + cz, :, g * 128 : g * 128 + 128
                    ]
    along_z = dot(rows[...], fz[...]).astype(BF)
    for yg in range(16):
        wide[:, yg * 128 : yg * 128 + 128] = along_z[yg * 128 : yg * 128 + 128]
    along_y = dot(wide[...], ky[...]).astype(BF)
    parents = [dot(scale, along_y[k * 64 : k * 64 + 64]).astype(BF) for k in range(2)]
    out[...] = parents[0]
    low_x[...] = mine[0, :4]
    high_x[...] = mine[0, 4:]

    def fill(first, second):
        for i in range(4):
            up[i] = (mine, other)[first][0, 2 * i + 1]
            dn[i] = (mine, other)[second][0, 2 * i]
        up[4] = parents[first]
        dn[4] = parents[second]

    @pl.when(where[2] == 0)
    def _():
        fill(0, 1)

    @pl.when(where[2] != 0)
    def _():
        fill(1, 0)


def prepare(where, fine_coeffs, s):
    def whole(*shape):
        return pl.BlockSpec(shape, lambda i, w: (0,) * len(shape))

    shapes = [(32, 1024), (4, 32, 1024), (4, 32, 1024), (5, 32, 1024), (5, 32, 1024), (256, 128), (2048, 1024), (64, 64)]
    return pl.pallas_call(
        prepare_kernel,
        out_shape=tuple(jax.ShapeDtypeStruct(shape, BF) for shape in shapes),
        grid_spec=pltpu.PrefetchScalarGridSpec(
            num_scalar_prefetch=1,
            grid=(1,),
            in_specs=[
                pl.BlockSpec((1, 8, 32, 1024), lambda i, w: (w[0], 0, 0, 0)),
                pl.BlockSpec((1, 8, 32, 1024), lambda i, w: (w[1], 0, 0, 0)),
                whole(32, 64),
            ],
            out_specs=[whole(*shape) for shape in shapes],
            scratch_shapes=[pltpu.VMEM((2048, 256), BF), pltpu.VMEM((128, 2048), BF)],
        ),
        interpret=INTERPRET,
        name="prepare",
        **grant(24),
    )(where, fine_coeffs, fine_coeffs, s)


PITCH_U = 68
PITCH_CU = 36
PITCH_CV = 100


def fill_left(left, sources, row):
    for zb in range(4):
        for g in range(8):
            left[row + g * 64 : row + g * 64 + 32, zb * 128 : zb * 128 + 128] = sources[zb][:, g * 128 : g * 128 + 128]


def inner_kernel(low_x, high_x, zm, zp, wz, mid, left):
    for cy in range(2):
        for cx in range(2):
            own = high_x if cx else low_x
            fill_left(left, [zm[2 * cx + cy], own[2 * cy], own[2 * cy + 1], zp[2 * cx + cy]], cy * 512 + cx * 32)

    def term(t, carry):
        weight = wz[t]
        for m in range(2):
            passed = dot(left[m * 512 : m * 512 + 512, :], weight).astype(BF)
            mid[t, m * 8 : m * 8 + 8] = passed.reshape(8, 64, 256)
        return carry

    lax.fori_loop(0, 8, term, 0)


def inner_pass(*operands):
    return call(inner_kernel, jax.ShapeDtypeStruct((8, 16, 64, 256), BF), [pltpu.VMEM((1024, 512), BF)])(*operands)


def fold_rows(passed, done, start, pitch):
    for i in range(4):
        lanes = passed[:, i * 128 : i * 128 + 128]
        done[pl.ds(start + i * pitch, 64), :] = lanes[:64] + pltpu.roll(lanes[64:], 64, 1)


def gather_lanes(done, first, g, cz, lane):
    block = None
    for j in range(4):
        part = done[pl.ds(first + 4 * g + j, 64, stride=PITCH_U), :]
        turn = (32 * (j - cz)) % 128
        moved = pltpu.roll(part, turn, 1) if turn else part
        block = moved if block is None else jnp.where(lane == j, moved, block)
    return block


def outer_kernel(
    inner, xm_own, xp_own, xm_far, xp_far, wz, wx, my,
    send_up, send_dn, packed,
    left, mid_a, mid_b, wide, done,
):
    for cy in range(2):
        own = 2 * cy
        fill_left(left, [xm_far[cy], xm_own[own], xm_own[own + 1], xm_far[2 + cy]], cy * 512)
        fill_left(left, [xp_far[cy], xp_own[own], xp_own[own + 1], xp_far[2 + cy]], cy * 512 + 32)

    def along_z(t, mid):
        weight = wz[t]
        for m in range(2):
            passed = dot(left[m * 512 : m * 512 + 512, :], weight).astype(BF)
            mid[m * 8 : m * 8 + 8] = passed.reshape(8, 64, 256)

    def along_x(t, mid):
        weight_x = wx[t]
        start = pl.multiple_of(t * (32 * PITCH_U), 8)
        for yg in range(16):
            data = jnp.concatenate([mid[yg, :32], inner[t, yg], mid[yg, 32:]], axis=0)
            passed = dot(weight_x, data)
            wide[pl.ds(start + 2 * yg * PITCH_U, 64), :] = passed[:, :128]
            wide[pl.ds(start + (2 * yg + 1) * PITCH_U, 64), :] = passed[:, 128:]

    along_z(0, mid_a)

    def terms(k, carry):
        along_z(2 * k + 1, mid_b)
        along_x(2 * k, mid_a)
        along_z(2 * k + 2, mid_a)
        along_x(2 * k + 1, mid_b)
        return carry

    lax.fori_loop(0, 3, terms, 0)
    along_z(7, mid_b)
    along_x(6, mid_a)
    along_x(7, mid_b)

    def rows(step, carry):
        for k in (2 * step, 2 * step + 1):
            data = jnp.concatenate(
                [wide[pl.ds(4 * k + i, 256, stride=PITCH_U), :].astype(BF) for i in range(4)], axis=1
            )
            packed[k] = data
            fold_rows(dot(my[0], data), done, pl.multiple_of(k * (4 * PITCH_U), 8), PITCH_U)
        return carry

    lax.fori_loop(0, 8, rows, 0)

    lane = lax.broadcasted_iota(jnp.int32, (64, 128), 1) // 32

    def relay(step, carry):
        for g in (2 * step, 2 * step + 1):
            at = pl.multiple_of(g * 128, 128)
            for side in range(2):
                target = send_up if side else send_dn
                for cz in range(2):
                    block = gather_lanes(done, side * 32, g, cz, lane).astype(BF)
                    for cx in range(2):
                        target[2 * cx + cz, :, pl.ds(at, 128)] = block[cx * 32 : cx * 32 + 32]
        return carry

    lax.fori_loop(0, 4, relay, 0)


def outer_passes(*operands):
    return call(
        outer_kernel,
        (
            jax.ShapeDtypeStruct((4, 32, 1024), BF),
            jax.ShapeDtypeStruct((4, 32, 1024), BF),
            jax.ShapeDtypeStruct((16, 256, 512), BF),
        ),
        [
            pltpu.VMEM((1024, 512), BF),
            pltpu.VMEM((16, 64, 256), BF),
            pltpu.VMEM((16, 64, 256), BF),
            pltpu.VMEM((256 * PITCH_U, 128), F32),
            pltpu.VMEM((64 * PITCH_U, 128), F32),
        ],
    )(*operands)


def own_kernel(packed, my, out, done):
    def rows(k, carry):
        fold_rows(dot(my[1], packed[k]), done, pl.multiple_of(k * (4 * PITCH_U), 8), PITCH_U)
        return carry

    lax.fori_loop(0, 16, rows, 0)

    lane = lax.broadcasted_iota(jnp.int32, (64, 128), 1) // 32

    def relay(g, carry):
        at = pl.multiple_of(g * 128, 128)
        for cy in range(2):
            for cz in range(2):
                block = gather_lanes(done, cy * 32, g, cz, lane)
                for cx in range(2):
                    out[4 * cx + 2 * cy + cz, :, pl.ds(at, 128)] = block[cx * 32 : cx * 32 + 32]
        return carry

    lax.fori_loop(0, 8, relay, 0)


def own_rows(*operands):
    return call(own_kernel, jax.ShapeDtypeStruct((8, 32, 1024), F32), [pltpu.VMEM((64 * PITCH_U, 128), F32)])(*operands)


def coarse_kernel(
    par, zm, zp, xm, xp, wz, wx, my, fine_up, fine_dn,
    out, send_up, send_dn,
    left, mid_a, mid_b, wide, done,
):
    send_up[:4] = fine_up[...]
    send_dn[:4] = fine_dn[...]
    sources = [
        [xm[1], xm[0], xm[2]],
        [zm[4], par[...], zp[4]],
        [xp[1], xp[0], xp[2]],
    ]
    for xb in range(3):
        for zb in range(3):
            for g in range(8):
                row = g * 96 + xb * 32
                left[row : row + 32, zb * 128 : zb * 128 + 128] = sources[xb][zb][:, g * 128 : g * 128 + 128]

    def along_z(h, mid):
        weight = jnp.concatenate([wz[2 * h], wz[2 * h + 1]], axis=1)
        mid[...] = dot(left[...], weight).astype(BF).reshape(8, 96, 256)

    def along_x(h, mid):
        for i in range(2):
            weight_x = wx[2 * h + i]
            for g in range(0, 8, 2):
                data = jnp.concatenate(
                    [mid[g, :, i * 128 : i * 128 + 128], mid[g + 1, :, i * 128 : i * 128 + 128]], axis=1
                )
                moved = dot(weight_x, data)
                row = (h * 16 + i * 8 + g) * PITCH_CU
                wide[row : row + 32, :] = moved[:, :128]
                wide[row + PITCH_CU : row + PITCH_CU + 32, :] = moved[:, 128:]

    mids = (mid_a, mid_b)
    along_z(0, mid_a)
    for h in range(4):
        if h < 3:
            along_z(h + 1, mids[(h + 1) % 2])
        along_x(h, mids[h % 2])

    def rows(k, carry):
        data = jnp.concatenate(
            [wide[pl.ds(4 * k + i, 64, stride=PITCH_CU), :].astype(BF) for i in range(4)], axis=1
        )
        passed = dot(my[...], data)
        start = pl.multiple_of(k * (4 * PITCH_CV), 8)
        for i in range(4):
            lanes = passed[:, i * 128 : i * 128 + 128]
            total = lanes[:96]
            for j in range(1, 4):
                total = total + pltpu.roll(lanes[j * 96 : j * 96 + 96], 128 - 32 * j, 1)
            done[pl.ds(start + i * PITCH_CV, 96), :] = total
        return carry

    lax.fori_loop(0, 8, rows, 0)

    lane = lax.broadcasted_iota(jnp.int32, (32, 128), 1) // 32

    def relay(g, carry):
        at = pl.multiple_of(g * 128, 128)
        for vb in range(3):
            block = done[pl.ds(vb * 32 + 4 * g, 32, stride=PITCH_CV), :]
            for j in range(1, 4):
                part = done[pl.ds(vb * 32 + 4 * g + j, 32, stride=PITCH_CV), :]
                block = jnp.where(lane == j, pltpu.roll(part, 32 * j, 1), block)
            if vb == 0:
                send_dn[4, :, pl.ds(at, 128)] = block.astype(BF)
            elif vb == 2:
                send_up[4, :, pl.ds(at, 128)] = block.astype(BF)
            else:
                out[:, pl.ds(at, 128)] = block
        return carry

    lax.fori_loop(0, 8, relay, 0)


def coarse_passes(*operands):
    return call(
        coarse_kernel,
        (
            jax.ShapeDtypeStruct((32, 1024), F32),
            jax.ShapeDtypeStruct((5, 32, 1024), BF),
            jax.ShapeDtypeStruct((5, 32, 1024), BF),
        ),
        [
            pltpu.VMEM((768, 384), BF),
            pltpu.VMEM((8, 96, 256), BF),
            pltpu.VMEM((8, 96, 256), BF),
            pltpu.VMEM((64 * PITCH_CU, 128), F32),
            pltpu.VMEM((32 * PITCH_CV, 128), F32),
        ],
    )(*operands)


def final_kernel(own, own_c, low, high, fz, ky, st2, out, rows, mixed, deep):
    total = own_c[...] + low[4].astype(F32) + high[4].astype(F32)
    hi, lo = split(total)
    for g in range(8):
        rows[g * 64 : g * 64 + 32, :] = hi[:, g * 128 : g * 128 + 128]
        rows[g * 64 + 32 : g * 64 + 64, :] = lo[:, g * 128 : g * 128 + 128]
    along_z = dot_t(rows[...], fz[...])
    for g in range(8):
        both = along_z[g * 64 : g * 64 + 32] + along_z[g * 64 + 32 : g * 64 + 64]
        hi, lo = split(both)
        for cz in range(2):
            mixed[cz * 64 : cz * 64 + 32, g * 128 : g * 128 + 128] = hi[:, cz * 128 : cz * 128 + 128]
            mixed[cz * 64 + 32 : cz * 64 + 64, g * 128 : g * 128 + 128] = lo[:, cz * 128 : cz * 128 + 128]
    along_y = dot_t(mixed[...], ky[...])
    for cz in range(2):
        hi, lo = split(along_y[cz * 64 : cz * 64 + 32] + along_y[cz * 64 + 32 : cz * 64 + 64])
        deep[:32, :] = hi
        deep[32:, :] = lo
        along_x = dot(st2[...], deep[...])
        for cx in range(2):
            for cy in range(2):
                added = (low if cy == 0 else high)[2 * cx + cz].astype(F32)
                spread = along_x[cx * 32 : cx * 32 + 32, cy * 1024 : cy * 1024 + 1024]
                box = 4 * cx + 2 * cy + cz
                out[box] = (own[box] + spread + added).astype(BF)


def finish(*operands):
    return call(
        final_kernel,
        jax.ShapeDtypeStruct((8, 32, 1024), BF),
        [pltpu.VMEM((512, 128), BF), pltpu.VMEM((128, 1024), BF), pltpu.VMEM((64, 2048), BF)],
    )(*operands)


def shift(block, distance):
    count = lax.axis_size("box")
    return lax.ppermute(block, "box", [(i, (i + distance) % count) for i in range(count)])


def crosses(p, step):
    return (p % 2 == 1) if step == 1 else (p % 2 == 0)


def shift_z(block, step):
    boxes, groups = lax.axis_size("box"), lax.axis_size("term")
    route = []
    for p in range(boxes):
        for t in range(groups):
            to = groups - 1 - t if crosses(p, step) else t
            route.append((p * groups + t, ((p + step) % boxes) * groups + to))
    return lax.ppermute(block, ("box", "term"), route)


def in_hbm(array):
    return pltpu.with_memory_space_constraint(array, pltpu.HBM)


def steps(fine_coeffs, fine_blocks, coarse_blocks, two_scale, term_exponent):
    p = lax.axis_index("box")
    t = lax.axis_index("term")
    other = lax.axis_size("term") - 1 - t
    where = jnp.stack([t, other, p % 2]).astype(jnp.int32)
    par, low_x, high_x, up, dn, fz, ky, st2 = prepare(where, in_hbm(fine_coeffs), in_hbm(two_scale))
    zm = shift_z(up, 1)
    zp = shift_z(dn, -1)
    xm_own = shift(high_x, 16)
    xp_own = shift(low_x, -16)
    wz, wx, my, cwz, cwx, cmy = weights(term_exponent, fine_blocks, coarse_blocks)
    xm_far = shift(jnp.concatenate([zm[2:4], zp[2:4]], axis=0), 16)
    xp_far = shift(jnp.concatenate([zm[:2], zp[:2]], axis=0), -16)
    mid = inner_pass(low_x, high_x, zm, zp, wz)
    planes = jnp.stack([par, zm[4], zp[4]])
    cxm = shift(planes, 16)
    cxp = shift(planes, -16)

    send_up, send_dn, packed = outer_passes(mid, xm_own, xp_own, xm_far, xp_far, wz, wx, my)
    out_c, full_up, full_dn = coarse_passes(par, zm, zp, cxm, cxp, cwz, cwx, cmy, send_up, send_dn)
    low = shift(full_up, 4)
    high = shift(full_dn, -4)
    out = own_rows(packed, my)
    total = finish(out, out_c, low, high, fz, ky, st2)
    groups = lax.axis_size("term")
    mine = lax.all_to_all(total.reshape(groups, 2, 32, 1024), "term", 0, 0)
    return mine.astype(F32)


def solution(mesh):
    placed = (P(None, "box", None, None), P(), P(), P(), P())
    return jax.shard_map(
        steps,
        mesh=mesh,
        in_specs=placed,
        out_specs=P(None, ("box", "term"), None, None),
        check_vma=False,
    )
```

```python
import jax
import jax.numpy as jnp
from jax import lax
from jax.experimental import pallas as pl
from jax.experimental.pallas import tpu as pltpu
from jax.sharding import PartitionSpec as P


BF = jnp.bfloat16
F32 = jnp.float32
INTERPRET = False


def grant(mebibytes):
    return dict(compiler_params=pltpu.CompilerParams(vmem_limit_bytes=mebibytes * 1024 * 1024))


def dot(a, b):
    return jnp.dot(a, b, preferred_element_type=F32)


def dot_t(a, b):
    return lax.dot_general(a, b, (((1,), (1,)), ((), ())), preferred_element_type=F32)


def split(value):
    hi = value.astype(BF)
    return hi, (value - hi.astype(F32)).astype(BF)


def repeat(count, factor, body):
    def step(s, carry):
        for k in range(factor):
            body(s * factor + k)
        return carry

    lax.fori_loop(0, count // factor, step, 0)


def call(kernel, outs, scratch=(), size=24):
    return pl.pallas_call(kernel, out_shape=outs, scratch_shapes=list(scratch), interpret=INTERPRET, **grant(size))


def same(rows, columns, test):
    i = lax.broadcasted_iota(jnp.int32, (rows, columns), 0)
    j = lax.broadcasted_iota(jnp.int32, (rows, columns), 1)
    return test(i, j).astype(F32).astype(BF)


def weight_kernel(
    exponents, fine, coarse,
    wz, wx, my, cwz, cwx, cmy,
    dense, turned, tall, dense_c, turned_c, tall_c,
):
    wz[...] = jnp.zeros(wz.shape, BF)
    cwz[...] = jnp.zeros(cwz.shape, BF)
    dense[...] = jnp.zeros(dense.shape, F32)
    turned[...] = jnp.zeros(turned.shape, F32)
    eye = same(128, 128, lambda i, j: i == j)
    by_parity = same(64, 64, lambda i, j: j == 2 * (i % 32) + i // 32)
    by_four = same(32, 32, lambda i, j: j == 4 * (i % 8) + i // 8)

    def term(t, carry):
        e = exponents[t]
        for d in range(3):
            block = fine[e, d]
            for child in range(2):
                source = d + child
                for y in range(4):
                    row, column = source * 128 + y * 32, y * 64 + child * 32
                    wz[t, row : row + 32, column : column + 32] = block
                wide_block = block.astype(F32)
                dense[source * 32 : source * 32 + 32, child * 32 : child * 32 + 32] = wide_block
                target = 2 + child - d
                turned[child * 32 : child * 32 + 32, target * 32 : target * 32 + 32] = wide_block
        wx[t] = dot_t(eye[:64, :64], dense[...].astype(BF)).astype(BF)
        chosen = dot(by_parity, turned[...].astype(BF))
        for parity in range(2):
            tall[parity, pl.ds(t * 32, 32), :] = chosen[parity * 32 : parity * 32 + 32]
        for d in range(3):
            block = coarse[e, d]
            dense_c[d * 32 : d * 32 + 32, :] = block.astype(F32)
            turned_c[:, (2 - d) * 32 : (2 - d) * 32 + 32] = block.astype(F32)
            for y in range(4):
                cwz[t, d * 128 + y * 32 : d * 128 + y * 32 + 32, y * 32 : y * 32 + 32] = block
        cwx[t] = dot_t(eye[:32, :32], dense_c[...].astype(BF)).astype(BF)
        chosen = dot(by_four, turned_c[...].astype(BF))
        for parity in range(4):
            tall_c[parity, pl.ds(t * 8, 8), :] = chosen[parity * 8 : parity * 8 + 8]
        return carry

    lax.fori_loop(0, 8, term, 0)
    for parity in range(2):
        moved = dot_t(eye, tall[parity].astype(BF)).astype(BF)
        my[0, parity * 64 : parity * 64 + 32, :] = moved[:32]
        my[0, parity * 64 + 32 : parity * 64 + 64, :] = moved[96:]
        my[1, parity * 64 : parity * 64 + 64, :] = moved[32:96]
    for parity in range(4):
        cmy[parity * 96 : parity * 96 + 96, :] = dot_t(eye[:96, :96], tall_c[parity].astype(BF)).astype(BF)


def weights(exponents, fine, coarse):
    whole = pl.BlockSpec(memory_space=pltpu.VMEM)
    return pl.pallas_call(
        weight_kernel,
        out_shape=(
            jax.ShapeDtypeStruct((8, 512, 256), BF),
            jax.ShapeDtypeStruct((8, 64, 128), BF),
            jax.ShapeDtypeStruct((2, 128, 256), BF),
            jax.ShapeDtypeStruct((8, 384, 128), BF),
            jax.ShapeDtypeStruct((8, 32, 96), BF),
            jax.ShapeDtypeStruct((384, 64), BF),
        ),
        in_specs=[pl.BlockSpec(memory_space=pltpu.SMEM), whole, whole],
        scratch_shapes=[
            pltpu.VMEM((128, 64), F32),
            pltpu.VMEM((64, 128), F32),
            pltpu.VMEM((2, 256, 128), F32),
            pltpu.VMEM((96, 32), F32),
            pltpu.VMEM((32, 96), F32),
            pltpu.VMEM((4, 64, 96), F32),
        ],
        interpret=INTERPRET,
        name="weights",
        **grant(16),
    )(exponents, fine, coarse)


def prepare_kernel(where, mine, other, s, out, low_x, high_x, up, dn, fz, ky, st2, rows, wide):
    scale = s[...]
    tiled = lax.dot_general(
        scale, same(32, 128, lambda i, j: j % 32 == i), (((0,), (0,)), ((), ())), preferred_element_type=F32
    )
    block = same(128, 128, lambda i, j: i // 32 == j // 32).astype(F32)
    for cz in range(2):
        part = tiled[cz * 32 : cz * 32 + 32]
        fz[cz * 128 : cz * 128 + 128, :] = (jnp.concatenate([part] * 4, axis=0) * block).astype(BF)
    st2[...] = lax.dot_general(
        scale, same(32, 64, lambda i, j: j % 32 == i), (((0,), (0,)), ((), ())), preferred_element_type=F32
    ).astype(BF)
    spread = lax.dot_general(
        scale, same(32, 1024, lambda i, j: j // 32 == i), (((0,), (0,)), ((), ())), preferred_element_type=F32
    )
    mask = same(32, 1024, lambda i, j: j % 32 == i)
    for y in range(64):
        line = jnp.broadcast_to(spread[y : y + 1], (16, 1024)).astype(BF)
        ky[y * 32 : y * 32 + 16, :] = line * mask[:16]
        ky[y * 32 + 16 : y * 32 + 32, :] = line * mask[16:]
    for yg in range(16):
        cy, g = divmod(yg, 8)
        for k, boxes in enumerate((mine, other)):
            for cx in range(2):
                for cz in range(2):
                    row = yg * 128 + k * 64 + cx * 32
                    rows[row : row + 32, cz * 128 : cz * 128 + 128] = boxes[
                        0, 4 * cx + 2 * cy + cz, :, g * 128 : g * 128 + 128
                    ]
    along_z = dot(rows[...], fz[...]).astype(BF)
    for yg in range(16):
        wide[:, yg * 128 : yg * 128 + 128] = along_z[yg * 128 : yg * 128 + 128]
    along_y = dot(wide[...], ky[...]).astype(BF)
    parents = [dot(scale, along_y[k * 64 : k * 64 + 64]).astype(BF) for k in range(2)]
    out[...] = parents[0]
    low_x[...] = mine[0, :4]
    high_x[...] = mine[0, 4:]

    def fill(first, second):
        for i in range(4):
            up[i] = (mine, other)[first][0, 2 * i + 1]
            dn[i] = (mine, other)[second][0, 2 * i]
        up[4] = parents[first]
        dn[4] = parents[second]

    @pl.when(where[2] == 0)
    def _():
        fill(0, 1)

    @pl.when(where[2] != 0)
    def _():
        fill(1, 0)


def prepare(where, fine_coeffs, s):
    def whole(*shape):
        return pl.BlockSpec(shape, lambda i, w: (0,) * len(shape))

    shapes = [(32, 1024), (4, 32, 1024), (4, 32, 1024), (5, 32, 1024), (5, 32, 1024), (256, 128), (2048, 1024), (64, 64)]
    return pl.pallas_call(
        prepare_kernel,
        out_shape=tuple(jax.ShapeDtypeStruct(shape, BF) for shape in shapes),
        grid_spec=pltpu.PrefetchScalarGridSpec(
            num_scalar_prefetch=1,
            grid=(1,),
            in_specs=[
                pl.BlockSpec((1, 8, 32, 1024), lambda i, w: (w[0], 0, 0, 0)),
                pl.BlockSpec((1, 8, 32, 1024), lambda i, w: (w[1], 0, 0, 0)),
                whole(32, 64),
            ],
            out_specs=[whole(*shape) for shape in shapes],
            scratch_shapes=[pltpu.VMEM((2048, 256), BF), pltpu.VMEM((128, 2048), BF)],
        ),
        interpret=INTERPRET,
        name="prepare",
        **grant(24),
    )(where, fine_coeffs, fine_coeffs, s)


PITCH_U = 68
PITCH_CU = 36
PITCH_CV = 100


def fill_left(left, sources, row):
    for zb in range(4):
        for g in range(8):
            left[row + g * 64 : row + g * 64 + 32, zb * 128 : zb * 128 + 128] = sources[zb][:, g * 128 : g * 128 + 128]


def inner_kernel(low_x, high_x, zm, zp, wz, mid, left):
    for cy in range(2):
        for cx in range(2):
            own = high_x if cx else low_x
            fill_left(left, [zm[2 * cx + cy], own[2 * cy], own[2 * cy + 1], zp[2 * cx + cy]], cy * 512 + cx * 32)

    def term(t):
        weight = wz[t]
        for m in range(2):
            passed = dot(left[m * 512 : m * 512 + 512, :], weight).astype(BF)
            mid[t, m * 8 : m * 8 + 8] = passed.reshape(8, 64, 256)

    repeat(8, 2, term)


def inner_pass(*operands):
    return call(inner_kernel, jax.ShapeDtypeStruct((8, 16, 64, 256), BF), [pltpu.VMEM((1024, 512), BF)])(*operands)


def fold_rows(passed, done, start, pitch):
    for i in range(4):
        lanes = passed[:, i * 128 : i * 128 + 128]
        done[pl.ds(start + i * pitch, 64), :] = lanes[:64] + pltpu.roll(lanes[64:], 64, 1)


def gather_lanes(done, first, g, cz, lane):
    block = None
    for j in range(4):
        part = done[pl.ds(first + 4 * g + j, 64, stride=PITCH_U), :]
        turn = (32 * (j - cz)) % 128
        moved = pltpu.roll(part, turn, 1) if turn else part
        block = moved if block is None else jnp.where(lane == j, moved, block)
    return block


def outer_kernel(
    inner, xm_own, xp_own, xm_far, xp_far, wz, wx, my,
    send_up, send_dn, packed,
    left, mid_a, mid_b, wide, done,
):
    for cy in range(2):
        own = 2 * cy
        fill_left(left, [xm_far[cy], xm_own[own], xm_own[own + 1], xm_far[2 + cy]], cy * 512)
        fill_left(left, [xp_far[cy], xp_own[own], xp_own[own + 1], xp_far[2 + cy]], cy * 512 + 32)

    def along_z(t, mid):
        weight = wz[t]
        for m in range(2):
            passed = dot(left[m * 512 : m * 512 + 512, :], weight).astype(BF)
            mid[m * 8 : m * 8 + 8] = passed.reshape(8, 64, 256)

    def along_x(t, mid):
        weight_x = wx[t]
        start = pl.multiple_of(t * (32 * PITCH_U), 8)
        for yg in range(16):
            data = jnp.concatenate([mid[yg, :32], inner[t, yg], mid[yg, 32:]], axis=0)
            passed = dot(weight_x, data)
            wide[pl.ds(start + 2 * yg * PITCH_U, 64), :] = passed[:, :128]
            wide[pl.ds(start + (2 * yg + 1) * PITCH_U, 64), :] = passed[:, 128:]

    along_z(0, mid_a)

    def terms(k, carry):
        along_z(2 * k + 1, mid_b)
        along_x(2 * k, mid_a)
        along_z(2 * k + 2, mid_a)
        along_x(2 * k + 1, mid_b)
        return carry

    lax.fori_loop(0, 3, terms, 0)
    along_z(7, mid_b)
    along_x(6, mid_a)
    along_x(7, mid_b)

    def rows(k):
        data = jnp.concatenate(
            [wide[pl.ds(4 * k + i, 256, stride=PITCH_U), :].astype(BF) for i in range(4)], axis=1
        )
        packed[k] = data
        fold_rows(dot(my[0], data), done, pl.multiple_of(k * (4 * PITCH_U), 8), PITCH_U)

    repeat(16, 4, rows)

    lane = lax.broadcasted_iota(jnp.int32, (64, 128), 1) // 32

    def relay(g):
        at = pl.multiple_of(g * 128, 128)
        for side in range(2):
            target = send_up if side else send_dn
            for cz in range(2):
                block = gather_lanes(done, side * 32, g, cz, lane).astype(BF)
                for cx in range(2):
                    target[2 * cx + cz, :, pl.ds(at, 128)] = block[cx * 32 : cx * 32 + 32]

    repeat(8, 4, relay)


def outer_passes(*operands):
    return call(
        outer_kernel,
        (
            jax.ShapeDtypeStruct((4, 32, 1024), BF),
            jax.ShapeDtypeStruct((4, 32, 1024), BF),
            jax.ShapeDtypeStruct((16, 256, 512), BF),
        ),
        [
            pltpu.VMEM((1024, 512), BF),
            pltpu.VMEM((16, 64, 256), BF),
            pltpu.VMEM((16, 64, 256), BF),
            pltpu.VMEM((256 * PITCH_U, 128), F32),
            pltpu.VMEM((64 * PITCH_U, 128), F32),
        ],
    )(*operands)


def own_kernel(packed, my, out, done):
    def rows(k):
        fold_rows(dot(my[1], packed[k]), done, pl.multiple_of(k * (4 * PITCH_U), 8), PITCH_U)

    repeat(16, 4, rows)

    lane = lax.broadcasted_iota(jnp.int32, (64, 128), 1) // 32

    def relay(g):
        at = pl.multiple_of(g * 128, 128)
        for cy in range(2):
            for cz in range(2):
                block = gather_lanes(done, cy * 32, g, cz, lane)
                for cx in range(2):
                    out[4 * cx + 2 * cy + cz, :, pl.ds(at, 128)] = block[cx * 32 : cx * 32 + 32]

    repeat(8, 4, relay)


def own_rows(*operands):
    return call(own_kernel, jax.ShapeDtypeStruct((8, 32, 1024), F32), [pltpu.VMEM((64 * PITCH_U, 128), F32)])(*operands)


def coarse_kernel(
    par, zm, zp, xm, xp, wz, wx, my, fine_up, fine_dn,
    out, send_up, send_dn,
    left, mid_a, mid_b, wide, done,
):
    send_up[:4] = fine_up[...]
    send_dn[:4] = fine_dn[...]
    sources = [
        [xm[1], xm[0], xm[2]],
        [zm[4], par[...], zp[4]],
        [xp[1], xp[0], xp[2]],
    ]
    for xb in range(3):
        for zb in range(3):
            for g in range(8):
                row = g * 96 + xb * 32
                left[row : row + 32, zb * 128 : zb * 128 + 128] = sources[xb][zb][:, g * 128 : g * 128 + 128]

    def along_z(h, mid):
        weight = jnp.concatenate([wz[2 * h], wz[2 * h + 1]], axis=1)
        mid[...] = dot(left[...], weight).astype(BF).reshape(8, 96, 256)

    def along_x(h, mid):
        for i in range(2):
            weight_x = wx[2 * h + i]
            for g in range(0, 8, 2):
                data = jnp.concatenate(
                    [mid[g, :, i * 128 : i * 128 + 128], mid[g + 1, :, i * 128 : i * 128 + 128]], axis=1
                )
                moved = dot(weight_x, data)
                row = (h * 16 + i * 8 + g) * PITCH_CU
                wide[row : row + 32, :] = moved[:, :128]
                wide[row + PITCH_CU : row + PITCH_CU + 32, :] = moved[:, 128:]

    mids = (mid_a, mid_b)
    along_z(0, mid_a)
    for h in range(4):
        if h < 3:
            along_z(h + 1, mids[(h + 1) % 2])
        along_x(h, mids[h % 2])

    def rows(k):
        data = jnp.concatenate(
            [wide[pl.ds(4 * k + i, 64, stride=PITCH_CU), :].astype(BF) for i in range(4)], axis=1
        )
        passed = dot(my[...], data)
        start = pl.multiple_of(k * (4 * PITCH_CV), 8)
        for i in range(4):
            lanes = passed[:, i * 128 : i * 128 + 128]
            total = lanes[:96]
            for j in range(1, 4):
                total = total + pltpu.roll(lanes[j * 96 : j * 96 + 96], 128 - 32 * j, 1)
            done[pl.ds(start + i * PITCH_CV, 96), :] = total

    repeat(8, 4, rows)

    lane = lax.broadcasted_iota(jnp.int32, (32, 128), 1) // 32

    def relay(g):
        at = pl.multiple_of(g * 128, 128)
        for vb in range(3):
            block = done[pl.ds(vb * 32 + 4 * g, 32, stride=PITCH_CV), :]
            for j in range(1, 4):
                part = done[pl.ds(vb * 32 + 4 * g + j, 32, stride=PITCH_CV), :]
                block = jnp.where(lane == j, pltpu.roll(part, 32 * j, 1), block)
            if vb == 0:
                send_dn[4, :, pl.ds(at, 128)] = block.astype(BF)
            elif vb == 2:
                send_up[4, :, pl.ds(at, 128)] = block.astype(BF)
            else:
                out[:, pl.ds(at, 128)] = block

    repeat(8, 8, relay)


def coarse_passes(*operands):
    return call(
        coarse_kernel,
        (
            jax.ShapeDtypeStruct((32, 1024), F32),
            jax.ShapeDtypeStruct((5, 32, 1024), BF),
            jax.ShapeDtypeStruct((5, 32, 1024), BF),
        ),
        [
            pltpu.VMEM((768, 384), BF),
            pltpu.VMEM((8, 96, 256), BF),
            pltpu.VMEM((8, 96, 256), BF),
            pltpu.VMEM((64 * PITCH_CU, 128), F32),
            pltpu.VMEM((32 * PITCH_CV, 128), F32),
        ],
    )(*operands)


def final_kernel(own, own_c, low, high, fz, ky, st2, out, rows, mixed, deep):
    total = own_c[...] + low[4].astype(F32) + high[4].astype(F32)
    hi, lo = split(total)
    for g in range(8):
        rows[g * 64 : g * 64 + 32, :] = hi[:, g * 128 : g * 128 + 128]
        rows[g * 64 + 32 : g * 64 + 64, :] = lo[:, g * 128 : g * 128 + 128]
    along_z = dot_t(rows[...], fz[...])
    for g in range(8):
        both = along_z[g * 64 : g * 64 + 32] + along_z[g * 64 + 32 : g * 64 + 64]
        hi, lo = split(both)
        for cz in range(2):
            mixed[cz * 64 : cz * 64 + 32, g * 128 : g * 128 + 128] = hi[:, cz * 128 : cz * 128 + 128]
            mixed[cz * 64 + 32 : cz * 64 + 64, g * 128 : g * 128 + 128] = lo[:, cz * 128 : cz * 128 + 128]
    along_y = dot_t(mixed[...], ky[...])
    for cz in range(2):
        hi, lo = split(along_y[cz * 64 : cz * 64 + 32] + along_y[cz * 64 + 32 : cz * 64 + 64])
        deep[:32, :] = hi
        deep[32:, :] = lo
        along_x = dot(st2[...], deep[...])
        for cx in range(2):
            for cy in range(2):
                added = (low if cy == 0 else high)[2 * cx + cz].astype(F32)
                spread = along_x[cx * 32 : cx * 32 + 32, cy * 1024 : cy * 1024 + 1024]
                box = 4 * cx + 2 * cy + cz
                out[box] = (own[box] + spread + added).astype(BF)


def finish(*operands):
    return call(
        final_kernel,
        jax.ShapeDtypeStruct((8, 32, 1024), BF),
        [pltpu.VMEM((512, 128), BF), pltpu.VMEM((128, 1024), BF), pltpu.VMEM((64, 2048), BF)],
    )(*operands)


def shift(block, distance):
    count = lax.axis_size("box")
    return lax.ppermute(block, "box", [(i, (i + distance) % count) for i in range(count)])


def crosses(p, step):
    return (p % 2 == 1) if step == 1 else (p % 2 == 0)


def shift_z(block, step):
    boxes, groups = lax.axis_size("box"), lax.axis_size("term")
    route = []
    for p in range(boxes):
        for t in range(groups):
            to = groups - 1 - t if crosses(p, step) else t
            route.append((p * groups + t, ((p + step) % boxes) * groups + to))
    return lax.ppermute(block, ("box", "term"), route)


def in_hbm(array):
    return pltpu.with_memory_space_constraint(array, pltpu.HBM)


def steps(fine_coeffs, fine_blocks, coarse_blocks, two_scale, term_exponent):
    p = lax.axis_index("box")
    t = lax.axis_index("term")
    other = lax.axis_size("term") - 1 - t
    where = jnp.stack([t, other, p % 2]).astype(jnp.int32)
    par, low_x, high_x, up, dn, fz, ky, st2 = prepare(where, in_hbm(fine_coeffs), in_hbm(two_scale))
    zm = shift_z(up, 1)
    zp = shift_z(dn, -1)
    xm_own = shift(high_x, 16)
    xp_own = shift(low_x, -16)
    wz, wx, my, cwz, cwx, cmy = weights(term_exponent, fine_blocks, coarse_blocks)
    xm_far = shift(jnp.concatenate([zm[2:4], zp[2:4]], axis=0), 16)
    xp_far = shift(jnp.concatenate([zm[:2], zp[:2]], axis=0), -16)
    mid = inner_pass(low_x, high_x, zm, zp, wz)
    planes = jnp.stack([par, zm[4], zp[4]])
    cxm = shift(planes, 16)
    cxp = shift(planes, -16)

    send_up, send_dn, packed = outer_passes(mid, xm_own, xp_own, xm_far, xp_far, wz, wx, my)
    out_c, full_up, full_dn = coarse_passes(par, zm, zp, cxm, cxp, cwz, cwx, cmy, send_up, send_dn)
    low = shift(full_up, 4)
    high = shift(full_dn, -4)
    out = own_rows(packed, my)
    total = finish(out, out_c, low, high, fz, ky, st2)
    groups = lax.axis_size("term")
    mine = lax.all_to_all(total.reshape(groups, 2, 32, 1024), "term", 0, 0)
    return mine.astype(F32)


def solution(mesh):
    placed = (P(None, "box", None, None), P(), P(), P(), P())
    return jax.shard_map(
        steps,
        mesh=mesh,
        in_specs=placed,
        out_specs=P(None, ("box", "term"), None, None),
        check_vma=False,
    )
```

```python
import jax
import jax.numpy as jnp
from jax import lax
from jax.experimental import pallas as pl
from jax.experimental.pallas import tpu as pltpu
from jax.sharding import PartitionSpec as P


BF = jnp.bfloat16
F32 = jnp.float32
INTERPRET = False


def grant(mebibytes):
    return dict(compiler_params=pltpu.CompilerParams(vmem_limit_bytes=mebibytes * 1024 * 1024))


def dot(a, b):
    return jnp.dot(a, b, preferred_element_type=F32)


def dot_t(a, b):
    return lax.dot_general(a, b, (((1,), (1,)), ((), ())), preferred_element_type=F32)


def split(value):
    hi = value.astype(BF)
    return hi, (value - hi.astype(F32)).astype(BF)


def repeat(count, factor, body):
    def step(s, carry):
        for k in range(factor):
            body(s * factor + k)
        return carry

    lax.fori_loop(0, count // factor, step, 0)


def call(kernel, outs, scratch=(), size=24):
    return pl.pallas_call(kernel, out_shape=outs, scratch_shapes=list(scratch), interpret=INTERPRET, **grant(size))


def same(rows, columns, test):
    i = lax.broadcasted_iota(jnp.int32, (rows, columns), 0)
    j = lax.broadcasted_iota(jnp.int32, (rows, columns), 1)
    return test(i, j).astype(F32).astype(BF)


def weight_kernel(
    exponents, fine, coarse,
    wz, wx, my, cwz, cwx, cmy,
    dense, turned, tall, dense_c, turned_c, tall_c,
):
    wz[...] = jnp.zeros(wz.shape, BF)
    cwz[...] = jnp.zeros(cwz.shape, BF)
    dense[...] = jnp.zeros(dense.shape, F32)
    turned[...] = jnp.zeros(turned.shape, F32)
    eye = same(128, 128, lambda i, j: i == j)
    by_parity = same(64, 64, lambda i, j: j == 2 * (i % 32) + i // 32)
    by_four = same(32, 32, lambda i, j: j == 4 * (i % 8) + i // 8)

    def term(t, carry):
        e = exponents[t]
        for d in range(3):
            block = fine[e, d]
            for child in range(2):
                source = d + child
                for y in range(4):
                    row, column = source * 128 + y * 32, y * 64 + child * 32
                    wz[t, row : row + 32, column : column + 32] = block
                wide_block = block.astype(F32)
                dense[source * 32 : source * 32 + 32, child * 32 : child * 32 + 32] = wide_block
                target = 2 + child - d
                turned[child * 32 : child * 32 + 32, target * 32 : target * 32 + 32] = wide_block
        wx[t] = dot_t(eye[:64, :64], dense[...].astype(BF)).astype(BF)
        chosen = dot(by_parity, turned[...].astype(BF))
        for parity in range(2):
            tall[parity, pl.ds(t * 32, 32), :] = chosen[parity * 32 : parity * 32 + 32]
        for d in range(3):
            block = coarse[e, d]
            dense_c[d * 32 : d * 32 + 32, :] = block.astype(F32)
            turned_c[:, (2 - d) * 32 : (2 - d) * 32 + 32] = block.astype(F32)
            for y in range(4):
                cwz[t, d * 128 + y * 32 : d * 128 + y * 32 + 32, y * 32 : y * 32 + 32] = block
        cwx[t] = dot_t(eye[:32, :32], dense_c[...].astype(BF)).astype(BF)
        chosen = dot(by_four, turned_c[...].astype(BF))
        for parity in range(4):
            tall_c[parity, pl.ds(t * 8, 8), :] = chosen[parity * 8 : parity * 8 + 8]
        return carry

    lax.fori_loop(0, 8, term, 0)
    for parity in range(2):
        moved = dot_t(eye, tall[parity].astype(BF)).astype(BF)
        my[0, parity * 64 : parity * 64 + 32, :] = moved[:32]
        my[0, parity * 64 + 32 : parity * 64 + 64, :] = moved[96:]
        my[1, parity * 64 : parity * 64 + 64, :] = moved[32:96]
    for parity in range(4):
        cmy[parity * 96 : parity * 96 + 96, :] = dot_t(eye[:96, :96], tall_c[parity].astype(BF)).astype(BF)


def weights(exponents, fine, coarse):
    whole = pl.BlockSpec(memory_space=pltpu.VMEM)
    return pl.pallas_call(
        weight_kernel,
        out_shape=(
            jax.ShapeDtypeStruct((8, 512, 256), BF),
            jax.ShapeDtypeStruct((8, 64, 128), BF),
            jax.ShapeDtypeStruct((2, 128, 256), BF),
            jax.ShapeDtypeStruct((8, 384, 128), BF),
            jax.ShapeDtypeStruct((8, 32, 96), BF),
            jax.ShapeDtypeStruct((384, 64), BF),
        ),
        in_specs=[pl.BlockSpec(memory_space=pltpu.SMEM), whole, whole],
        scratch_shapes=[
            pltpu.VMEM((128, 64), F32),
            pltpu.VMEM((64, 128), F32),
            pltpu.VMEM((2, 256, 128), F32),
            pltpu.VMEM((96, 32), F32),
            pltpu.VMEM((32, 96), F32),
            pltpu.VMEM((4, 64, 96), F32),
        ],
        interpret=INTERPRET,
        name="weights",
        **grant(16),
    )(exponents, fine, coarse)


def prepare_kernel(where, boxes_in, s, out, low_x, high_x, up, dn, fz, ky, st2, rows, wide, mine, other, filters, arrived):
    copies = [
        pltpu.make_async_copy(boxes_in.at[where[k]], target, arrived.at[k]) for k, target in enumerate((mine, other))
    ]
    for copy in copies:
        copy.start()
    first = pltpu.make_async_copy(s, filters, arrived.at[2])
    first.start()
    first.wait()
    scale = filters[...]
    tiled = lax.dot_general(
        scale, same(32, 128, lambda i, j: j % 32 == i), (((0,), (0,)), ((), ())), preferred_element_type=F32
    )
    block = same(128, 128, lambda i, j: i // 32 == j // 32).astype(F32)
    for cz in range(2):
        part = tiled[cz * 32 : cz * 32 + 32]
        fz[cz * 128 : cz * 128 + 128, :] = (jnp.concatenate([part] * 4, axis=0) * block).astype(BF)
    st2[...] = lax.dot_general(
        scale, same(32, 64, lambda i, j: j % 32 == i), (((0,), (0,)), ((), ())), preferred_element_type=F32
    ).astype(BF)
    spread = lax.dot_general(
        scale, same(32, 1024, lambda i, j: j // 32 == i), (((0,), (0,)), ((), ())), preferred_element_type=F32
    )
    mask = same(32, 1024, lambda i, j: j % 32 == i)
    for y in range(64):
        line = jnp.broadcast_to(spread[y : y + 1], (16, 1024)).astype(BF)
        ky[y * 32 : y * 32 + 16, :] = line * mask[:16]
        ky[y * 32 + 16 : y * 32 + 32, :] = line * mask[16:]
    for copy in copies:
        copy.wait()
    for yg in range(16):
        cy, g = divmod(yg, 8)
        for k, boxes in enumerate((mine, other)):
            for cx in range(2):
                for cz in range(2):
                    row = yg * 128 + k * 64 + cx * 32
                    rows[row : row + 32, cz * 128 : cz * 128 + 128] = boxes[
                        4 * cx + 2 * cy + cz, :, g * 128 : g * 128 + 128
                    ]
    along_z = dot(rows[...], fz[...]).astype(BF)
    for yg in range(16):
        wide[:, yg * 128 : yg * 128 + 128] = along_z[yg * 128 : yg * 128 + 128]
    along_y = dot(wide[...], ky[...]).astype(BF)
    parents = [dot(scale, along_y[k * 64 : k * 64 + 64]).astype(BF) for k in range(2)]
    out[...] = parents[0]
    low_x[...] = mine[:4]
    high_x[...] = mine[4:]

    def fill(first, second):
        for i in range(4):
            up[i] = (mine, other)[first][2 * i + 1]
            dn[i] = (mine, other)[second][2 * i]
        up[4] = parents[first]
        dn[4] = parents[second]

    @pl.when(where[2] == 0)
    def _():
        fill(0, 1)

    @pl.when(where[2] != 0)
    def _():
        fill(1, 0)


def prepare(where, fine_coeffs, s):
    shapes = [(32, 1024), (4, 32, 1024), (4, 32, 1024), (5, 32, 1024), (5, 32, 1024), (256, 128), (2048, 1024), (64, 64)]
    return pl.pallas_call(
        prepare_kernel,
        out_shape=tuple(jax.ShapeDtypeStruct(shape, BF) for shape in shapes),
        in_specs=[
            pl.BlockSpec(memory_space=pltpu.SMEM),
            pl.BlockSpec(memory_space=pl.ANY),
            pl.BlockSpec(memory_space=pl.ANY),
        ],
        scratch_shapes=[
            pltpu.VMEM((2048, 256), BF),
            pltpu.VMEM((128, 2048), BF),
            pltpu.VMEM((8, 32, 1024), BF),
            pltpu.VMEM((8, 32, 1024), BF),
            pltpu.VMEM((32, 64), BF),
            pltpu.SemaphoreType.DMA((3,)),
        ],
        interpret=INTERPRET,
        name="prepare",
        **grant(24),
    )(where, fine_coeffs, s)


PITCH_U = 68
PITCH_CU = 36
PITCH_CV = 100


def fill_left(left, sources, row):
    for zb in range(4):
        for g in range(8):
            left[row + g * 64 : row + g * 64 + 32, zb * 128 : zb * 128 + 128] = sources[zb][:, g * 128 : g * 128 + 128]


def inner_kernel(low_x, high_x, zm, zp, wz, mid, left):
    for cy in range(2):
        for cx in range(2):
            own = high_x if cx else low_x
            fill_left(left, [zm[2 * cx + cy], own[2 * cy], own[2 * cy + 1], zp[2 * cx + cy]], cy * 512 + cx * 32)

    def term(t):
        weight = wz[t]
        for m in range(2):
            passed = dot(left[m * 512 : m * 512 + 512, :], weight).astype(BF)
            mid[t, m * 8 : m * 8 + 8] = passed.reshape(8, 64, 256)

    repeat(8, 2, term)


def inner_pass(*operands):
    return call(inner_kernel, jax.ShapeDtypeStruct((8, 16, 64, 256), BF), [pltpu.VMEM((1024, 512), BF)])(*operands)


def fold_rows(passed, done, start, pitch):
    for i in range(4):
        lanes = passed[:, i * 128 : i * 128 + 128]
        done[pl.ds(start + i * pitch, 64), :] = lanes[:64] + pltpu.roll(lanes[64:], 64, 1)


def gather_lanes(done, first, g, cz, lane):
    block = None
    for j in range(4):
        part = done[pl.ds(first + 4 * g + j, 64, stride=PITCH_U), :]
        turn = (32 * (j - cz)) % 128
        moved = pltpu.roll(part, turn, 1) if turn else part
        block = moved if block is None else jnp.where(lane == j, moved, block)
    return block


def outer_kernel(
    inner, xm_own, xp_own, xm_far, xp_far, wz, wx, my,
    send_up, send_dn, packed,
    left, mid_a, mid_b, wide, done,
):
    for cy in range(2):
        own = 2 * cy
        fill_left(left, [xm_far[cy], xm_own[own], xm_own[own + 1], xm_far[2 + cy]], cy * 512)
        fill_left(left, [xp_far[cy], xp_own[own], xp_own[own + 1], xp_far[2 + cy]], cy * 512 + 32)

    def along_z(t, mid):
        weight = wz[t]
        for m in range(2):
            passed = dot(left[m * 512 : m * 512 + 512, :], weight).astype(BF)
            mid[m * 8 : m * 8 + 8] = passed.reshape(8, 64, 256)

    def along_x(t, mid):
        weight_x = wx[t]
        start = pl.multiple_of(t * (32 * PITCH_U), 8)
        for yg in range(16):
            data = jnp.concatenate([mid[yg, :32], inner[t, yg], mid[yg, 32:]], axis=0)
            passed = dot(weight_x, data)
            wide[pl.ds(start + 2 * yg * PITCH_U, 64), :] = passed[:, :128]
            wide[pl.ds(start + (2 * yg + 1) * PITCH_U, 64), :] = passed[:, 128:]

    along_z(0, mid_a)

    def terms(k, carry):
        along_z(2 * k + 1, mid_b)
        along_x(2 * k, mid_a)
        along_z(2 * k + 2, mid_a)
        along_x(2 * k + 1, mid_b)
        return carry

    lax.fori_loop(0, 3, terms, 0)
    along_z(7, mid_b)
    along_x(6, mid_a)
    along_x(7, mid_b)

    def rows(k):
        data = jnp.concatenate(
            [wide[pl.ds(4 * k + i, 256, stride=PITCH_U), :].astype(BF) for i in range(4)], axis=1
        )
        packed[k] = data
        fold_rows(dot(my[0], data), done, pl.multiple_of(k * (4 * PITCH_U), 8), PITCH_U)

    repeat(16, 4, rows)

    lane = lax.broadcasted_iota(jnp.int32, (64, 128), 1) // 32

    def relay(g):
        at = pl.multiple_of(g * 128, 128)
        for side in range(2):
            target = send_up if side else send_dn
            for cz in range(2):
                block = gather_lanes(done, side * 32, g, cz, lane).astype(BF)
                for cx in range(2):
                    target[2 * cx + cz, :, pl.ds(at, 128)] = block[cx * 32 : cx * 32 + 32]

    repeat(8, 4, relay)


def outer_passes(*operands):
    return call(
        outer_kernel,
        (
            jax.ShapeDtypeStruct((4, 32, 1024), BF),
            jax.ShapeDtypeStruct((4, 32, 1024), BF),
            jax.ShapeDtypeStruct((16, 256, 512), BF),
        ),
        [
            pltpu.VMEM((1024, 512), BF),
            pltpu.VMEM((16, 64, 256), BF),
            pltpu.VMEM((16, 64, 256), BF),
            pltpu.VMEM((256 * PITCH_U, 128), F32),
            pltpu.VMEM((64 * PITCH_U, 128), F32),
        ],
    )(*operands)


def own_kernel(packed, my, out, done):
    def rows(k):
        fold_rows(dot(my[1], packed[k]), done, pl.multiple_of(k * (4 * PITCH_U), 8), PITCH_U)

    repeat(16, 4, rows)

    lane = lax.broadcasted_iota(jnp.int32, (64, 128), 1) // 32

    def relay(g):
        at = pl.multiple_of(g * 128, 128)
        for cy in range(2):
            for cz in range(2):
                block = gather_lanes(done, cy * 32, g, cz, lane)
                for cx in range(2):
                    out[4 * cx + 2 * cy + cz, :, pl.ds(at, 128)] = block[cx * 32 : cx * 32 + 32]

    repeat(8, 4, relay)


def own_rows(*operands):
    return call(own_kernel, jax.ShapeDtypeStruct((8, 32, 1024), F32), [pltpu.VMEM((64 * PITCH_U, 128), F32)])(*operands)


def coarse_kernel(
    par, zm, zp, xm, xp, wz, wx, my, fine_up, fine_dn,
    out, send_up, send_dn,
    left, mid_a, mid_b, wide, done,
):
    send_up[:4] = fine_up[...]
    send_dn[:4] = fine_dn[...]
    sources = [
        [xm[1], xm[0], xm[2]],
        [zm[4], par[...], zp[4]],
        [xp[1], xp[0], xp[2]],
    ]
    for xb in range(3):
        for zb in range(3):
            for g in range(8):
                row = g * 96 + xb * 32
                left[row : row + 32, zb * 128 : zb * 128 + 128] = sources[xb][zb][:, g * 128 : g * 128 + 128]

    def along_z(h, mid):
        weight = jnp.concatenate([wz[2 * h], wz[2 * h + 1]], axis=1)
        mid[...] = dot(left[...], weight).astype(BF).reshape(8, 96, 256)

    def along_x(h, mid):
        for i in range(2):
            weight_x = wx[2 * h + i]
            for g in range(0, 8, 2):
                data = jnp.concatenate(
                    [mid[g, :, i * 128 : i * 128 + 128], mid[g + 1, :, i * 128 : i * 128 + 128]], axis=1
                )
                moved = dot(weight_x, data)
                row = (h * 16 + i * 8 + g) * PITCH_CU
                wide[row : row + 32, :] = moved[:, :128]
                wide[row + PITCH_CU : row + PITCH_CU + 32, :] = moved[:, 128:]

    mids = (mid_a, mid_b)
    along_z(0, mid_a)
    for h in range(4):
        if h < 3:
            along_z(h + 1, mids[(h + 1) % 2])
        along_x(h, mids[h % 2])

    def rows(k):
        data = jnp.concatenate(
            [wide[pl.ds(4 * k + i, 64, stride=PITCH_CU), :].astype(BF) for i in range(4)], axis=1
        )
        passed = dot(my[...], data)
        start = pl.multiple_of(k * (4 * PITCH_CV), 8)
        for i in range(4):
            lanes = passed[:, i * 128 : i * 128 + 128]
            total = lanes[:96]
            for j in range(1, 4):
                total = total + pltpu.roll(lanes[j * 96 : j * 96 + 96], 128 - 32 * j, 1)
            done[pl.ds(start + i * PITCH_CV, 96), :] = total

    repeat(8, 4, rows)

    lane = lax.broadcasted_iota(jnp.int32, (32, 128), 1) // 32

    def relay(g):
        at = pl.multiple_of(g * 128, 128)
        for vb in range(3):
            block = done[pl.ds(vb * 32 + 4 * g, 32, stride=PITCH_CV), :]
            for j in range(1, 4):
                part = done[pl.ds(vb * 32 + 4 * g + j, 32, stride=PITCH_CV), :]
                block = jnp.where(lane == j, pltpu.roll(part, 32 * j, 1), block)
            if vb == 0:
                send_dn[4, :, pl.ds(at, 128)] = block.astype(BF)
            elif vb == 2:
                send_up[4, :, pl.ds(at, 128)] = block.astype(BF)
            else:
                out[:, pl.ds(at, 128)] = block

    repeat(8, 8, relay)


def coarse_passes(*operands):
    return call(
        coarse_kernel,
        (
            jax.ShapeDtypeStruct((32, 1024), F32),
            jax.ShapeDtypeStruct((5, 32, 1024), BF),
            jax.ShapeDtypeStruct((5, 32, 1024), BF),
        ),
        [
            pltpu.VMEM((768, 384), BF),
            pltpu.VMEM((8, 96, 256), BF),
            pltpu.VMEM((8, 96, 256), BF),
            pltpu.VMEM((64 * PITCH_CU, 128), F32),
            pltpu.VMEM((32 * PITCH_CV, 128), F32),
        ],
    )(*operands)


def final_kernel(own, own_c, low, high, fz, ky, st2, out, rows, mixed, deep):
    total = own_c[...] + low[4].astype(F32) + high[4].astype(F32)
    hi, lo = split(total)
    for g in range(8):
        rows[g * 64 : g * 64 + 32, :] = hi[:, g * 128 : g * 128 + 128]
        rows[g * 64 + 32 : g * 64 + 64, :] = lo[:, g * 128 : g * 128 + 128]
    along_z = dot_t(rows[...], fz[...])
    for g in range(8):
        both = along_z[g * 64 : g * 64 + 32] + along_z[g * 64 + 32 : g * 64 + 64]
        hi, lo = split(both)
        for cz in range(2):
            mixed[cz * 64 : cz * 64 + 32, g * 128 : g * 128 + 128] = hi[:, cz * 128 : cz * 128 + 128]
            mixed[cz * 64 + 32 : cz * 64 + 64, g * 128 : g * 128 + 128] = lo[:, cz * 128 : cz * 128 + 128]
    along_y = dot_t(mixed[...], ky[...])
    for cz in range(2):
        hi, lo = split(along_y[cz * 64 : cz * 64 + 32] + along_y[cz * 64 + 32 : cz * 64 + 64])
        deep[:32, :] = hi
        deep[32:, :] = lo
        along_x = dot(st2[...], deep[...])
        for cx in range(2):
            for cy in range(2):
                added = (low if cy == 0 else high)[2 * cx + cz].astype(F32)
                spread = along_x[cx * 32 : cx * 32 + 32, cy * 1024 : cy * 1024 + 1024]
                box = 4 * cx + 2 * cy + cz
                out[box] = (own[box] + spread + added).astype(BF)


def finish(*operands):
    return call(
        final_kernel,
        jax.ShapeDtypeStruct((8, 32, 1024), BF),
        [pltpu.VMEM((512, 128), BF), pltpu.VMEM((128, 1024), BF), pltpu.VMEM((64, 2048), BF)],
    )(*operands)


def shift(block, distance):
    count = lax.axis_size("box")
    return lax.ppermute(block, "box", [(i, (i + distance) % count) for i in range(count)])


def crosses(p, step):
    return (p % 2 == 1) if step == 1 else (p % 2 == 0)


def shift_z(block, step):
    boxes, groups = lax.axis_size("box"), lax.axis_size("term")
    route = []
    for p in range(boxes):
        for t in range(groups):
            to = groups - 1 - t if crosses(p, step) else t
            route.append((p * groups + t, ((p + step) % boxes) * groups + to))
    return lax.ppermute(block, ("box", "term"), route)


def in_hbm(array):
    return pltpu.with_memory_space_constraint(array, pltpu.HBM)


def steps(fine_coeffs, fine_blocks, coarse_blocks, two_scale, term_exponent):
    p = lax.axis_index("box")
    t = lax.axis_index("term")
    other = lax.axis_size("term") - 1 - t
    where = jnp.stack([t, other, p % 2]).astype(jnp.int32)
    par, low_x, high_x, up, dn, fz, ky, st2 = prepare(where, in_hbm(fine_coeffs), in_hbm(two_scale))
    zm = shift_z(up, 1)
    zp = shift_z(dn, -1)
    xm_own = shift(high_x, 16)
    xp_own = shift(low_x, -16)
    wz, wx, my, cwz, cwx, cmy = weights(term_exponent, fine_blocks, coarse_blocks)
    xm_far = shift(jnp.concatenate([zm[2:4], zp[2:4]], axis=0), 16)
    xp_far = shift(jnp.concatenate([zm[:2], zp[:2]], axis=0), -16)
    mid = inner_pass(low_x, high_x, zm, zp, wz)
    planes = jnp.stack([par, zm[4], zp[4]])
    cxm = shift(planes, 16)
    cxp = shift(planes, -16)

    send_up, send_dn, packed = outer_passes(mid, xm_own, xp_own, xm_far, xp_far, wz, wx, my)
    out_c, full_up, full_dn = coarse_passes(par, zm, zp, cxm, cxp, cwz, cwx, cmy, send_up, send_dn)
    low = shift(full_up, 4)
    high = shift(full_dn, -4)
    out = own_rows(packed, my)
    total = finish(out, out_c, low, high, fz, ky, st2)
    groups = lax.axis_size("term")
    mine = lax.all_to_all(total.reshape(groups, 2, 32, 1024), "term", 0, 0)
    return mine.astype(F32)


def solution(mesh):
    placed = (P(None, "box", None, None), P(), P(), P(), P())
    return jax.shard_map(
        steps,
        mesh=mesh,
        in_specs=placed,
        out_specs=P(None, ("box", "term"), None, None),
        check_vma=False,
    )
```

```python
import jax
import jax.numpy as jnp
from jax import lax
from jax.experimental import pallas as pl
from jax.experimental.pallas import tpu as pltpu
from jax.sharding import PartitionSpec as P


BF = jnp.bfloat16
F32 = jnp.float32
INTERPRET = False


def grant(mebibytes):
    return dict(compiler_params=pltpu.CompilerParams(vmem_limit_bytes=mebibytes * 1024 * 1024))


def dot(a, b):
    return jnp.dot(a, b, preferred_element_type=F32)


def dot_t(a, b):
    return lax.dot_general(a, b, (((1,), (1,)), ((), ())), preferred_element_type=F32)


def split(value):
    hi = value.astype(BF)
    return hi, (value - hi.astype(F32)).astype(BF)


def repeat(count, factor, body):
    def step(s, carry):
        for k in range(factor):
            body(s * factor + k)
        return carry

    lax.fori_loop(0, count // factor, step, 0)


def call(kernel, outs, scratch=(), size=24):
    return pl.pallas_call(kernel, out_shape=outs, scratch_shapes=list(scratch), interpret=INTERPRET, **grant(size))


def same(rows, columns, test):
    i = lax.broadcasted_iota(jnp.int32, (rows, columns), 0)
    j = lax.broadcasted_iota(jnp.int32, (rows, columns), 1)
    return test(i, j).astype(F32).astype(BF)


def weight_kernel(
    exponents, fine, coarse,
    wz, wx, my, cwz, cwx, cmy,
    dense, turned, tall, dense_c, turned_c, tall_c,
):
    wz[...] = jnp.zeros(wz.shape, BF)
    cwz[...] = jnp.zeros(cwz.shape, BF)
    dense[...] = jnp.zeros(dense.shape, F32)
    turned[...] = jnp.zeros(turned.shape, F32)
    eye = same(128, 128, lambda i, j: i == j)
    by_parity = same(64, 64, lambda i, j: j == 2 * (i % 32) + i // 32)
    by_four = same(32, 32, lambda i, j: j == 4 * (i % 8) + i // 8)

    def term(t, carry):
        e = exponents[t]
        for d in range(3):
            block = fine[e, d]
            for child in range(2):
                source = d + child
                for y in range(4):
                    row, column = source * 128 + y * 32, y * 64 + child * 32
                    wz[t, row : row + 32, column : column + 32] = block
                wide_block = block.astype(F32)
                dense[source * 32 : source * 32 + 32, child * 32 : child * 32 + 32] = wide_block
                target = 2 + child - d
                turned[child * 32 : child * 32 + 32, target * 32 : target * 32 + 32] = wide_block
        wx[t] = dot_t(eye[:64, :64], dense[...].astype(BF)).astype(BF)
        chosen = dot(by_parity, turned[...].astype(BF))
        for parity in range(2):
            tall[parity, pl.ds(t * 32, 32), :] = chosen[parity * 32 : parity * 32 + 32]
        for d in range(3):
            block = coarse[e, d]
            dense_c[d * 32 : d * 32 + 32, :] = block.astype(F32)
            turned_c[:, (2 - d) * 32 : (2 - d) * 32 + 32] = block.astype(F32)
            for y in range(4):
                cwz[t, d * 128 + y * 32 : d * 128 + y * 32 + 32, y * 32 : y * 32 + 32] = block
        cwx[t] = dot_t(eye[:32, :32], dense_c[...].astype(BF)).astype(BF)
        chosen = dot(by_four, turned_c[...].astype(BF))
        for parity in range(4):
            tall_c[parity, pl.ds(t * 8, 8), :] = chosen[parity * 8 : parity * 8 + 8]
        return carry

    lax.fori_loop(0, 8, term, 0)
    for parity in range(2):
        moved = dot_t(eye, tall[parity].astype(BF)).astype(BF)
        my[0, parity * 64 : parity * 64 + 32, :] = moved[:32]
        my[0, parity * 64 + 32 : parity * 64 + 64, :] = moved[96:]
        my[1, parity * 64 : parity * 64 + 64, :] = moved[32:96]
    for parity in range(4):
        cmy[parity * 96 : parity * 96 + 96, :] = dot_t(eye[:96, :96], tall_c[parity].astype(BF)).astype(BF)


def weights(exponents, fine, coarse):
    whole = pl.BlockSpec(memory_space=pltpu.VMEM)
    return pl.pallas_call(
        weight_kernel,
        out_shape=(
            jax.ShapeDtypeStruct((8, 512, 256), BF),
            jax.ShapeDtypeStruct((8, 64, 128), BF),
            jax.ShapeDtypeStruct((2, 128, 256), BF),
            jax.ShapeDtypeStruct((8, 384, 128), BF),
            jax.ShapeDtypeStruct((8, 32, 96), BF),
            jax.ShapeDtypeStruct((384, 64), BF),
        ),
        in_specs=[pl.BlockSpec(memory_space=pltpu.SMEM), whole, whole],
        scratch_shapes=[
            pltpu.VMEM((128, 64), F32),
            pltpu.VMEM((64, 128), F32),
            pltpu.VMEM((2, 256, 128), F32),
            pltpu.VMEM((96, 32), F32),
            pltpu.VMEM((32, 96), F32),
            pltpu.VMEM((4, 64, 96), F32),
        ],
        interpret=INTERPRET,
        name="weights",
        **grant(16),
    )(exponents, fine, coarse)


def prepare_kernel(where, boxes_in, s, out, low_x, high_x, up, dn, fz, ky, st2, rows, wide, mine, other, filters, arrived):
    copies = [
        pltpu.make_async_copy(boxes_in.at[where[k]], target, arrived.at[k]) for k, target in enumerate((mine, other))
    ]
    for copy in copies:
        copy.start()
    first = pltpu.make_async_copy(s, filters, arrived.at[2])
    first.start()
    first.wait()
    scale = filters[...]
    tiled = lax.dot_general(
        scale, same(32, 128, lambda i, j: j % 32 == i), (((0,), (0,)), ((), ())), preferred_element_type=F32
    )
    block = same(128, 128, lambda i, j: i // 32 == j // 32).astype(F32)
    for cz in range(2):
        part = tiled[cz * 32 : cz * 32 + 32]
        fz[cz * 128 : cz * 128 + 128, :] = (jnp.concatenate([part] * 4, axis=0) * block).astype(BF)
    st2[...] = lax.dot_general(
        scale, same(32, 64, lambda i, j: j % 32 == i), (((0,), (0,)), ((), ())), preferred_element_type=F32
    ).astype(BF)
    spread = lax.dot_general(
        scale, same(32, 1024, lambda i, j: j // 32 == i), (((0,), (0,)), ((), ())), preferred_element_type=F32
    )
    mask = same(32, 1024, lambda i, j: j % 32 == i)
    for y in range(64):
        line = jnp.broadcast_to(spread[y : y + 1], (16, 1024)).astype(BF)
        ky[y * 32 : y * 32 + 16, :] = line * mask[:16]
        ky[y * 32 + 16 : y * 32 + 32, :] = line * mask[16:]
    for copy in copies:
        copy.wait()
    for yg in range(16):
        cy, g = divmod(yg, 8)
        for k, boxes in enumerate((mine, other)):
            for cx in range(2):
                for cz in range(2):
                    row = yg * 128 + k * 64 + cx * 32
                    rows[row : row + 32, cz * 128 : cz * 128 + 128] = boxes[
                        4 * cx + 2 * cy + cz, :, g * 128 : g * 128 + 128
                    ]
    along_z = dot(rows[...], fz[...]).astype(BF)
    for yg in range(16):
        wide[:, yg * 128 : yg * 128 + 128] = along_z[yg * 128 : yg * 128 + 128]
    along_y = dot(wide[...], ky[...]).astype(BF)
    parents = [dot(scale, along_y[k * 64 : k * 64 + 64]).astype(BF) for k in range(2)]
    out[...] = parents[0]
    low_x[...] = mine[:4]
    high_x[...] = mine[4:]

    def fill(first, second):
        for i in range(4):
            up[i] = (mine, other)[first][2 * i + 1]
            dn[i] = (mine, other)[second][2 * i]
        up[4] = parents[first]
        dn[4] = parents[second]

    @pl.when(where[2] == 0)
    def _():
        fill(0, 1)

    @pl.when(where[2] != 0)
    def _():
        fill(1, 0)


def prepare(where, fine_coeffs, s):
    shapes = [(32, 1024), (4, 32, 1024), (4, 32, 1024), (5, 32, 1024), (5, 32, 1024), (256, 128), (2048, 1024), (64, 64)]
    return pl.pallas_call(
        prepare_kernel,
        out_shape=tuple(jax.ShapeDtypeStruct(shape, BF) for shape in shapes),
        in_specs=[
            pl.BlockSpec(memory_space=pltpu.SMEM),
            pl.BlockSpec(memory_space=pl.ANY),
            pl.BlockSpec(memory_space=pl.ANY),
        ],
        scratch_shapes=[
            pltpu.VMEM((2048, 256), BF),
            pltpu.VMEM((128, 2048), BF),
            pltpu.VMEM((8, 32, 1024), BF),
            pltpu.VMEM((8, 32, 1024), BF),
            pltpu.VMEM((32, 64), BF),
            pltpu.SemaphoreType.DMA((3,)),
        ],
        interpret=INTERPRET,
        name="prepare",
        **grant(24),
    )(where, fine_coeffs, s)


PITCH_U = 68
PITCH_CU = 36


def fill_left(left, sources, row):
    for zb in range(4):
        for g in range(8):
            left[row + g * 64 : row + g * 64 + 32, zb * 128 : zb * 128 + 128] = sources[zb][:, g * 128 : g * 128 + 128]


def inner_kernel(low_x, high_x, zm, zp, wz, mid, left):
    for cy in range(2):
        for cx in range(2):
            own = high_x if cx else low_x
            fill_left(left, [zm[2 * cx + cy], own[2 * cy], own[2 * cy + 1], zp[2 * cx + cy]], cy * 512 + cx * 32)

    def term(t):
        weight = wz[t]
        for m in range(2):
            passed = dot(left[m * 512 : m * 512 + 512, :], weight).astype(BF)
            mid[t, m * 8 : m * 8 + 8] = passed.reshape(8, 64, 256)

    repeat(8, 2, term)


def inner_pass(*operands):
    return call(inner_kernel, jax.ShapeDtypeStruct((8, 16, 64, 256), BF), [pltpu.VMEM((1024, 512), BF)])(*operands)


def fold_rows(passed, done, start, pitch):
    for i in range(4):
        lanes = passed[:, i * 128 : i * 128 + 128]
        done[pl.ds(start + i * pitch, 64), :] = lanes[:64] + pltpu.roll(lanes[64:], 64, 1)


def gather_lanes(done, first, g, cz, lane):
    block = None
    for j in range(4):
        part = done[pl.ds(first + 4 * g + j, 64, stride=PITCH_U), :]
        turn = (32 * (j - cz)) % 128
        moved = pltpu.roll(part, turn, 1) if turn else part
        block = moved if block is None else jnp.where(lane == j, moved, block)
    return block


def outer_kernel(
    inner, xm_own, xp_own, xm_far, xp_far, wz, wx, my,
    send_up, send_dn, packed,
    left, mid_a, mid_b, wide, done,
):
    for cy in range(2):
        own = 2 * cy
        fill_left(left, [xm_far[cy], xm_own[own], xm_own[own + 1], xm_far[2 + cy]], cy * 512)
        fill_left(left, [xp_far[cy], xp_own[own], xp_own[own + 1], xp_far[2 + cy]], cy * 512 + 32)

    def along_z(t, mid):
        weight = wz[t]
        for m in range(2):
            passed = dot(left[m * 512 : m * 512 + 512, :], weight).astype(BF)
            mid[m * 8 : m * 8 + 8] = passed.reshape(8, 64, 256)

    def along_x(t, mid):
        weight_x = wx[t]
        start = pl.multiple_of(t * (32 * PITCH_U), 8)
        for yg in range(16):
            data = jnp.concatenate([mid[yg, :32], inner[t, yg], mid[yg, 32:]], axis=0)
            passed = dot(weight_x, data)
            wide[pl.ds(start + 2 * yg * PITCH_U, 64), :] = passed[:, :128]
            wide[pl.ds(start + (2 * yg + 1) * PITCH_U, 64), :] = passed[:, 128:]

    along_z(0, mid_a)

    def terms(k, carry):
        along_z(2 * k + 1, mid_b)
        along_x(2 * k, mid_a)
        along_z(2 * k + 2, mid_a)
        along_x(2 * k + 1, mid_b)
        return carry

    lax.fori_loop(0, 3, terms, 0)
    along_z(7, mid_b)
    along_x(6, mid_a)
    along_x(7, mid_b)

    def rows(k):
        data = jnp.concatenate(
            [wide[pl.ds(4 * k + i, 256, stride=PITCH_U), :].astype(BF) for i in range(4)], axis=1
        )
        packed[k] = data
        fold_rows(dot(my[0], data), done, pl.multiple_of(k * (4 * PITCH_U), 8), PITCH_U)

    repeat(16, 4, rows)

    lane = lax.broadcasted_iota(jnp.int32, (64, 128), 1) // 32

    def relay(g):
        at = pl.multiple_of(g * 128, 128)
        for side in range(2):
            target = send_up if side else send_dn
            for cz in range(2):
                block = gather_lanes(done, side * 32, g, cz, lane).astype(BF)
                for cx in range(2):
                    target[2 * cx + cz, :, pl.ds(at, 128)] = block[cx * 32 : cx * 32 + 32]

    repeat(8, 4, relay)


def outer_passes(*operands):
    return call(
        outer_kernel,
        (
            jax.ShapeDtypeStruct((4, 32, 1024), BF),
            jax.ShapeDtypeStruct((4, 32, 1024), BF),
            jax.ShapeDtypeStruct((16, 256, 512), BF),
        ),
        [
            pltpu.VMEM((1024, 512), BF),
            pltpu.VMEM((16, 64, 256), BF),
            pltpu.VMEM((16, 64, 256), BF),
            pltpu.VMEM((256 * PITCH_U, 128), F32),
            pltpu.VMEM((64 * PITCH_U, 128), F32),
        ],
    )(*operands)


def own_kernel(packed, my, packed_c, my_c, out, out_c, done, done_c):
    inner = jnp.concatenate([my_c[j * 96 + 32 : j * 96 + 64, :] for j in range(4)], axis=0)

    def rows_c(k):
        fold_four(dot(inner, packed_c[k]), done_c, pl.multiple_of(k * (4 * PITCH_CU), 8), PITCH_CU, 32)

    repeat(8, 4, rows_c)

    lane_c = lax.broadcasted_iota(jnp.int32, (32, 128), 1) // 32

    def relay_c(g):
        out_c[:, pl.ds(pl.multiple_of(g * 128, 128), 128)] = gather_four(done_c, 4 * g, PITCH_CU, lane_c)

    repeat(8, 8, relay_c)

    def rows(k):
        fold_rows(dot(my[1], packed[k]), done, pl.multiple_of(k * (4 * PITCH_U), 8), PITCH_U)

    repeat(16, 4, rows)

    lane = lax.broadcasted_iota(jnp.int32, (64, 128), 1) // 32

    def relay(g):
        at = pl.multiple_of(g * 128, 128)
        for cy in range(2):
            for cz in range(2):
                block = gather_lanes(done, cy * 32, g, cz, lane)
                for cx in range(2):
                    out[4 * cx + 2 * cy + cz, :, pl.ds(at, 128)] = block[cx * 32 : cx * 32 + 32]

    repeat(8, 4, relay)


def own_rows(*operands):
    return call(
        own_kernel,
        (jax.ShapeDtypeStruct((8, 32, 1024), F32), jax.ShapeDtypeStruct((32, 1024), F32)),
        [pltpu.VMEM((64 * PITCH_U, 128), F32), pltpu.VMEM((32 * PITCH_CU, 128), F32)],
    )(*operands)


def fold_four(passed, done, start, pitch, height):
    for i in range(4):
        lanes = passed[:, i * 128 : i * 128 + 128]
        total = lanes[:height]
        for j in range(1, 4):
            total = total + pltpu.roll(lanes[j * height : j * height + height], 128 - 32 * j, 1)
        done[pl.ds(start + i * pitch, height), :] = total


def gather_four(done, first, pitch, lane):
    block = done[pl.ds(first, 32, stride=pitch), :]
    for j in range(1, 4):
        part = done[pl.ds(first + j, 32, stride=pitch), :]
        block = jnp.where(lane == j, pltpu.roll(part, 32 * j, 1), block)
    return block


def coarse_kernel(
    par, zm, zp, xm, xp, wz, wx, my, fine_up, fine_dn,
    send_up, send_dn, packed,
    left, mid_a, mid_b, wide, done,
):
    send_up[:4] = fine_up[...]
    send_dn[:4] = fine_dn[...]
    sources = [
        [xm[1], xm[0], xm[2]],
        [zm[4], par[...], zp[4]],
        [xp[1], xp[0], xp[2]],
    ]
    for xb in range(3):
        for zb in range(3):
            for g in range(8):
                row = g * 96 + xb * 32
                left[row : row + 32, zb * 128 : zb * 128 + 128] = sources[xb][zb][:, g * 128 : g * 128 + 128]

    def along_z(h, mid):
        weight = jnp.concatenate([wz[2 * h], wz[2 * h + 1]], axis=1)
        mid[...] = dot(left[...], weight).astype(BF).reshape(8, 96, 256)

    def along_x(h, mid):
        for i in range(2):
            weight_x = wx[2 * h + i]
            for g in range(0, 8, 2):
                data = jnp.concatenate(
                    [mid[g, :, i * 128 : i * 128 + 128], mid[g + 1, :, i * 128 : i * 128 + 128]], axis=1
                )
                moved = dot(weight_x, data)
                row = (h * 16 + i * 8 + g) * PITCH_CU
                wide[row : row + 32, :] = moved[:, :128]
                wide[row + PITCH_CU : row + PITCH_CU + 32, :] = moved[:, 128:]

    mids = (mid_a, mid_b)
    along_z(0, mid_a)
    for h in range(4):
        if h < 3:
            along_z(h + 1, mids[(h + 1) % 2])
        along_x(h, mids[h % 2])

    outer = jnp.concatenate(
        [my[j * 96 + vb * 32 : j * 96 + vb * 32 + 32, :] for j in range(4) for vb in (0, 2)], axis=0
    )

    def rows(k):
        data = jnp.concatenate(
            [wide[pl.ds(4 * k + i, 64, stride=PITCH_CU), :].astype(BF) for i in range(4)], axis=1
        )
        packed[k] = data
        fold_four(dot(outer, data), done, pl.multiple_of(k * (4 * PITCH_U), 8), PITCH_U, 64)

    repeat(8, 4, rows)

    lane = lax.broadcasted_iota(jnp.int32, (32, 128), 1) // 32

    def relay(g):
        at = pl.multiple_of(g * 128, 128)
        for side, target in enumerate((send_dn, send_up)):
            target[4, :, pl.ds(at, 128)] = gather_four(done, side * 32 + 4 * g, PITCH_U, lane).astype(BF)

    repeat(8, 8, relay)


def coarse_passes(*operands):
    return call(
        coarse_kernel,
        (
            jax.ShapeDtypeStruct((5, 32, 1024), BF),
            jax.ShapeDtypeStruct((5, 32, 1024), BF),
            jax.ShapeDtypeStruct((8, 64, 512), BF),
        ),
        [
            pltpu.VMEM((768, 384), BF),
            pltpu.VMEM((8, 96, 256), BF),
            pltpu.VMEM((8, 96, 256), BF),
            pltpu.VMEM((64 * PITCH_CU, 128), F32),
            pltpu.VMEM((32 * PITCH_U, 128), F32),
        ],
    )(*operands)


def final_kernel(own, own_c, low, high, fz, ky, st2, out, rows, mixed, deep):
    total = own_c[...] + low[4].astype(F32) + high[4].astype(F32)
    hi, lo = split(total)
    for g in range(8):
        rows[g * 64 : g * 64 + 32, :] = hi[:, g * 128 : g * 128 + 128]
        rows[g * 64 + 32 : g * 64 + 64, :] = lo[:, g * 128 : g * 128 + 128]
    along_z = dot_t(rows[...], fz[...])
    for g in range(8):
        both = along_z[g * 64 : g * 64 + 32] + along_z[g * 64 + 32 : g * 64 + 64]
        hi, lo = split(both)
        for cz in range(2):
            mixed[cz * 64 : cz * 64 + 32, g * 128 : g * 128 + 128] = hi[:, cz * 128 : cz * 128 + 128]
            mixed[cz * 64 + 32 : cz * 64 + 64, g * 128 : g * 128 + 128] = lo[:, cz * 128 : cz * 128 + 128]
    along_y = dot_t(mixed[...], ky[...])
    for cz in range(2):
        hi, lo = split(along_y[cz * 64 : cz * 64 + 32] + along_y[cz * 64 + 32 : cz * 64 + 64])
        deep[:32, :] = hi
        deep[32:, :] = lo
        along_x = dot(st2[...], deep[...])
        for cx in range(2):
            for cy in range(2):
                added = (low if cy == 0 else high)[2 * cx + cz].astype(F32)
                spread = along_x[cx * 32 : cx * 32 + 32, cy * 1024 : cy * 1024 + 1024]
                box = 4 * cx + 2 * cy + cz
                out[box] = (own[box] + spread + added).astype(BF)


def finish(*operands):
    return call(
        final_kernel,
        jax.ShapeDtypeStruct((8, 32, 1024), BF),
        [pltpu.VMEM((512, 128), BF), pltpu.VMEM((128, 1024), BF), pltpu.VMEM((64, 2048), BF)],
    )(*operands)


def shift(block, distance):
    count = lax.axis_size("box")
    return lax.ppermute(block, "box", [(i, (i + distance) % count) for i in range(count)])


def crosses(p, step):
    return (p % 2 == 1) if step == 1 else (p % 2 == 0)


def shift_z(block, step):
    boxes, groups = lax.axis_size("box"), lax.axis_size("term")
    route = []
    for p in range(boxes):
        for t in range(groups):
            to = groups - 1 - t if crosses(p, step) else t
            route.append((p * groups + t, ((p + step) % boxes) * groups + to))
    return lax.ppermute(block, ("box", "term"), route)


def in_hbm(array):
    return pltpu.with_memory_space_constraint(array, pltpu.HBM)


def steps(fine_coeffs, fine_blocks, coarse_blocks, two_scale, term_exponent):
    p = lax.axis_index("box")
    t = lax.axis_index("term")
    other = lax.axis_size("term") - 1 - t
    where = jnp.stack([t, other, p % 2]).astype(jnp.int32)
    par, low_x, high_x, up, dn, fz, ky, st2 = prepare(where, in_hbm(fine_coeffs), in_hbm(two_scale))
    zm = shift_z(up, 1)
    zp = shift_z(dn, -1)
    xm_own = shift(high_x, 16)
    xp_own = shift(low_x, -16)
    wz, wx, my, cwz, cwx, cmy = weights(term_exponent, fine_blocks, coarse_blocks)
    xm_far = shift(jnp.concatenate([zm[2:4], zp[2:4]], axis=0), 16)
    xp_far = shift(jnp.concatenate([zm[:2], zp[:2]], axis=0), -16)
    mid = inner_pass(low_x, high_x, zm, zp, wz)
    planes = jnp.stack([par, zm[4], zp[4]])
    cxm = shift(planes, 16)
    cxp = shift(planes, -16)

    send_up, send_dn, packed = outer_passes(mid, xm_own, xp_own, xm_far, xp_far, wz, wx, my)
    full_up, full_dn, packed_c = coarse_passes(par, zm, zp, cxm, cxp, cwz, cwx, cmy, send_up, send_dn)
    low = shift(full_up, 4)
    high = shift(full_dn, -4)
    out, out_c = own_rows(packed, my, packed_c, cmy)
    total = finish(out, out_c, low, high, fz, ky, st2)
    groups = lax.axis_size("term")
    mine = lax.all_to_all(total.reshape(groups, 2, 32, 1024), "term", 0, 0)
    return mine.astype(F32)


def solution(mesh):
    placed = (P(None, "box", None, None), P(), P(), P(), P())
    return jax.shard_map(
        steps,
        mesh=mesh,
        in_specs=placed,
        out_specs=P(None, ("box", "term"), None, None),
        check_vma=False,
    )
```
